512 devices in a mesh: view: 32 (over y_lo, z), band: 4 (over x), batch: 4 (over y_hi, core).
Axes of the slice: x: 4, y: 4 (y_hi: 2, y_lo: 2; y = y_hi * 2 + y_lo), z: 16, core: 2. Of those that a mesh axis runs over, the one named last changes fastest.
Arguments:
- images: bfloat16 [128, 32, 16, 768], P(('batch', 'view'), 'band'), parts along dimension 0, may hold values from -6 to 6
- frame_gain: float32 [768], replicated, may hold values from 0.5 to 2.5
- frame_qkv: bfloat16 [768, 1536], replicated, may hold values from -0.3 to 0.3
- frame_out: bfloat16 [512, 768], replicated, may hold values from -0.25 to 0.25
- row1_gain: float32 [768], replicated, may hold values from 0.5 to 2.5
- row1_qkv: bfloat16 [768, 1536], P('band'), may hold values from -0.3 to 0.3
- row1_out: bfloat16 [512, 768], P(None, 'band'), may hold values from -0.25 to 0.25
- row2_gain: float32 [768], replicated, may hold values from 0.5 to 2.5
- row2_qkv: bfloat16 [768, 1536], P('band'), may hold values from -0.3 to 0.3
- row2_out: bfloat16 [512, 768], P(None, 'band'), may hold values from -0.25 to 0.25
Outputs:
- refined: bfloat16 [128, 32, 16, 768], P(('batch', 'view'), 'band'), parts along dimension 0
The draws below stay inside these ranges and needn't reach their ends.
There are 4 independent parts, one for each index of `batch`. The reference program is written for one: setup_inputs(seed, part) draws one part's arguments, and reference() takes and returns one part's arrays. A program takes and returns all parts, laid end to end along the dimension named above; an argument that names none is the same for every part. Nothing has to cross between parts.
All inputs are finite; a program needn't handle non-finite values.
Results may differ from the reference program's by a relative error of at most 0.02.
Values may be sent and summed in bfloat16 or wider, within the bound.
No kernel may reach another device: no remote copies, remote signals or barrier semaphores. Data moves between devices by JAX's collectives and lax.ppermute only.
A program may use at most 64 MiB of HBM per device.

```python
import jax
import jax.numpy as jnp
from jax import lax

D = 768
HEAD_DIM = 64
HEADS = 8
COLS = 16
VIEWS = 32
HEIGHT = 32
E = 512


def gain_values(key):
    return jax.random.uniform(key, (D,), minval=0.5, maxval=1.5)


def projection_values(key):
    inner = HEADS * HEAD_DIM
    query_key, key_key, value_key = jax.random.split(key, 3)
    spread = 1.4 * D ** (-0.5)
    queries = jax.random.normal(query_key, (D, inner)) * spread
    fresh = jax.random.normal(key_key, (D, inner)) * spread
    keys = fresh
    values = jax.random.normal(value_key, (D, inner)) * D ** (-0.5)
    return jnp.clip(jnp.concatenate([queries, keys, values], axis=1), -0.29, 0.29).astype(jnp.bfloat16)


def draw_images(key, part):
    key = jax.random.fold_in(key, 31)
    shape = (VIEWS, HEIGHT, COLS, D)
    base_key = jax.random.fold_in(key, 0)
    values = jax.random.normal(base_key, shape)
    return jnp.clip(values, -6.0, 6.0).astype(jnp.bfloat16)


def draw_frame_gain(key, part):
    return gain_values(jax.random.fold_in(key, 11))


def draw_row1_gain(key, part):
    return gain_values(jax.random.fold_in(key, 12))


def draw_row2_gain(key, part):
    return gain_values(jax.random.fold_in(key, 13))


def draw_frame_qkv(key, part):
    return projection_values(jax.random.fold_in(key, 21))


def draw_row1_qkv(key, part):
    return projection_values(jax.random.fold_in(key, 22))


def draw_row2_qkv(key, part):
    return projection_values(jax.random.fold_in(key, 23))


def block_levels(key, shape, shards, low, largest):
    loudness = 1.0
    for axis_at, parts in shards:
        heights = jax.random.uniform(jax.random.fold_in(jax.random.fold_in(key, 6), axis_at), (parts,), jnp.float32, low / len(shards), largest / len(shards))
        loudness = loudness * jnp.repeat(jnp.exp(heights), shape[axis_at] // parts).reshape((-1,) + (1,) * (len(shape) - 1 - axis_at))
    return loudness


def scatter_about(own_key, dims, deviation, most, cuts=(), kind=jnp.bfloat16):
    result = deviation * jax.random.normal(own_key, dims, jnp.float32)
    if cuts:
        result = result * block_levels(own_key, dims, cuts, -0.22, 0.18)
    return jnp.clip(result, -most, most).astype(kind)


def setup_inputs(seed: int = 0, part: int = 0) -> dict:
    splits = jax.random.split(jax.random.key(seed), 11)
    own_keys = jax.random.split(jax.random.fold_in(splits[10], part), 11)
    return {
        "images": draw_images(jax.random.fold_in(jax.random.fold_in(splits[10], part), 71), part),
        "frame_gain": draw_frame_gain(jax.random.fold_in(splits[10], 71), part),
        "frame_qkv": draw_frame_qkv(jax.random.fold_in(splits[10], 71), part),
        "frame_out": scatter_about(splits[3], (E, D), E ** -0.5, 0.25),
        "row1_gain": draw_row1_gain(jax.random.fold_in(splits[10], 71), part),
        "row1_qkv": draw_row1_qkv(jax.random.fold_in(splits[10], 71), part),
        "row1_out": scatter_about(splits[6], (E, D), E ** -0.5, 0.25, ((1, 4),)),
        "row2_gain": draw_row2_gain(jax.random.fold_in(splits[10], 71), part),
        "row2_qkv": draw_row2_qkv(jax.random.fold_in(splits[10], 71), part),
        "row2_out": scatter_about(splits[9], (E, D), E ** -0.5, 0.25, ((1, 4),)),
    }


def normalize(stream, gain):
    values = stream.astype(jnp.float32)
    factor = lax.rsqrt(lax.optimization_barrier(jnp.mean(values * values, axis=-1, keepdims=True)) + 1e-06)
    return (values * factor * gain).astype(jnp.bfloat16)

def attention(queries, keys, values):
    scores = jnp.einsum('qhd,khd->hqk', queries.astype(jnp.float32), keys.astype(jnp.float32)) * HEAD_DIM ** (-0.5)
    highest = lax.optimization_barrier(jnp.max(scores, axis=-1, keepdims=True))
    weights = jnp.exp(scores - highest)
    rounded = lax.optimization_barrier(weights.astype(jnp.bfloat16)).astype(jnp.float32)
    mixed = jnp.einsum('hqk,khd->qhd', rounded, values.astype(jnp.float32))
    total = jnp.transpose(lax.optimization_barrier(jnp.sum(weights, axis=-1)))
    return (mixed / total[:, :, None]).astype(jnp.bfloat16)

def project_attend(normed, qkv_weight, out_weight):
    tokens = normed.shape[0]
    inner = HEADS * HEAD_DIM
    triple = jnp.dot(normed, qkv_weight, preferred_element_type=jnp.float32).astype(jnp.bfloat16)
    triple = triple.reshape(tokens, 3, HEADS, HEAD_DIM)
    attended = attention(triple[:, 0], triple[:, 1], triple[:, 2]).reshape(tokens, inner)
    return jnp.dot(attended, out_weight, preferred_element_type=jnp.float32)

def row_layer(stream, gain, qkv_weight, out_weight):
    views, height, columns, width = stream.shape
    normed = normalize(stream, gain)
    rows_first = jnp.transpose(normed, (1, 0, 2, 3))

    def one_row(image_row):
        update = project_attend(image_row.reshape(views * columns, width), qkv_weight, out_weight)
        return update.reshape(views, columns, width)
    update = jnp.transpose(lax.map(one_row, rows_first), (1, 0, 2, 3))
    return (stream.astype(jnp.float32) + update).astype(jnp.bfloat16)

def reference(images, frame_gain, frame_qkv, frame_out, row1_gain, row1_qkv, row1_out, row2_gain, row2_qkv, row2_out):
    views, height, columns, width = images.shape
    normed = normalize(images, frame_gain)

    def one_view(frame):
        update = project_attend(frame.reshape(height * columns, width), frame_qkv, frame_out)
        return update.reshape(height, columns, width)
    update = lax.map(one_view, normed)
    stream = (images.astype(jnp.float32) + update).astype(jnp.bfloat16)
    stream = row_layer(stream, row1_gain, row1_qkv, row1_out)
    return row_layer(stream, row2_gain, row2_qkv, row2_out)
```

```python
import functools

import jax
import jax.numpy as jnp
from jax import lax
from jax.experimental import pallas as pl
from jax.experimental.pallas import tpu as pltpu
from jax.sharding import PartitionSpec as P

HEAD_DIM = 64
EPSILON = 1e-06
PAIR = 2 * HEAD_DIM


def normed_block(block, gain):
    values = block.astype(jnp.float32)
    factor = lax.rsqrt(jnp.mean(values * values, axis=-1, keepdims=True) + EPSILON)
    return (values * factor * gain).astype(jnp.bfloat16)


def attention_body(transposed_out, all_ref, own_ref, gain_ref, qkv_ref, out_ref, result_ref, kv_ref):
    chunks, tokens, width = all_ref.shape
    inner = kv_ref.shape[1] // 2
    gain = gain_ref[...]
    for chunk in range(chunks):
        normed = normed_block(all_ref[chunk], gain)
        kv_ref[chunk * tokens : (chunk + 1) * tokens, :] = jnp.dot(
            normed, qkv_ref[:, inner : 3 * inner], preferred_element_type=jnp.float32
        ).astype(jnp.bfloat16)
    own = own_ref[...]
    normed = normed_block(own, gain)
    queries = (
        jnp.dot(normed, qkv_ref[:, :inner], preferred_element_type=jnp.float32)
        .astype(jnp.bfloat16)
    ) * jnp.bfloat16(HEAD_DIM ** (-0.5))
    lane = lax.broadcasted_iota(jnp.int32, (tokens, PAIR), 1)
    first = lane < HEAD_DIM
    attended = []
    for pair in range(inner // PAIR):
        columns = slice(pair * PAIR, (pair + 1) * PAIR)
        query = queries[:, columns]
        keys = kv_ref[:, columns]
        values = kv_ref[:, inner + pair * PAIR : inner + (pair + 1) * PAIR]
        halves = []
        for mask in (first, jnp.logical_not(first)):
            masked = jnp.where(mask, query, jnp.zeros_like(query))
            scores = lax.dot_general(
                masked, keys, (((1,), (1,)), ((), ())), preferred_element_type=jnp.float32
            )
            highest = jnp.max(scores, axis=-1, keepdims=True)
            weights = jnp.exp(scores - highest)
            total = jnp.sum(weights, axis=-1, keepdims=True)
            mixed = jnp.dot(
                weights.astype(jnp.bfloat16), values, preferred_element_type=jnp.float32
            )
            halves.append(mixed / total)
        attended.append(jnp.where(first, halves[0], halves[1]).astype(jnp.bfloat16))
    attended = jnp.concatenate(attended, axis=1)
    contract = (((1,), (1,)), ((), ())) if transposed_out else (((1,), (0,)), ((), ()))
    update = lax.dot_general(
        attended, out_ref[...], contract, preferred_element_type=jnp.float32
    )
    stream = (own.astype(jnp.float32) + update).astype(jnp.bfloat16)
    if len(result_ref.shape) == 2:
        result_ref[...] = stream
    else:
        for copy in range(result_ref.shape[0]):
            result_ref[copy] = stream


def row_body(copies, all_ref, own_ref, gain_ref, weight_ref, result_ref, kv_ref):
    inner = kv_ref.shape[1] // 2
    attention_body(
        True,
        all_ref,
        own_ref,
        gain_ref,
        weight_ref.at[:, : 3 * inner],
        weight_ref.at[:, 3 * inner :],
        result_ref,
        kv_ref,
    )


def sublayer(everything, own, gain, weights, inner, name, copies=None):
    chunks, tokens, width = everything.shape
    shape = (tokens, width) if copies is None else (copies, tokens, width)
    body = (
        functools.partial(attention_body, False)
        if len(weights) == 2
        else functools.partial(row_body, copies)
    )
    count = chunks * tokens
    return pl.pallas_call(
        body,
        out_shape=jax.ShapeDtypeStruct(shape, jnp.bfloat16),
        in_specs=[pl.BlockSpec(memory_space=pltpu.VMEM)] * (3 + len(weights)),
        out_specs=pl.BlockSpec(memory_space=pltpu.VMEM),
        scratch_shapes=[pltpu.VMEM((count, 2 * inner), jnp.bfloat16)],
        compiler_params=pltpu.CompilerParams(vmem_limit_bytes=24 << 20),
        cost_estimate=pl.CostEstimate(
            flops=2 * count * width * 2 * inner + 4 * tokens * width * inner + 4 * tokens * count * inner,
            bytes_accessed=2 * (count * width + 4 * width * inner),
            transcendentals=tokens * count * inner // HEAD_DIM,
        ),
        name=name,
    )(everything, own, gain.reshape(1, width), *weights)


def gathered(stream, copies, axis, groups=None):
    return lax.all_to_all(
        jnp.broadcast_to(stream[None], (copies,) + stream.shape),
        axis,
        split_axis=0,
        concat_axis=0,
        tiled=True,
        axis_index_groups=groups,
    )


def local(
    images,
    frame_gain,
    frame_qkv,
    frame_out,
    row1_gain,
    row1_qkv,
    row1_out,
    row2_gain,
    row2_qkv,
    row2_out,
):
    _, row_count, col_count, width = images.shape
    inner = frame_out.shape[0]
    tokens = row_count * col_count
    views = lax.axis_size("view")
    bands = lax.axis_size("band")
    share = views // row_count
    near = 2
    deep = views // near
    side = share // near
    spread = [
        [y * deep + h * side + l for h in range(row_count)] for y in range(near) for l in range(side)
    ]
    ring = [
        [h * side + l for l in range(side)] + [deep + h * side + l for l in reversed(range(side))]
        for h in range(row_count)
    ]
    row1 = lax.all_gather(jnp.concatenate([row1_qkv, row1_out.T], axis=1), "band", axis=0, tiled=True)
    row2 = lax.all_gather(jnp.concatenate([row2_qkv, row2_out.T], axis=1), "band", axis=0, tiled=True)

    stream = images.reshape(tokens, width)
    everything = gathered(stream, bands, "band")
    stream = sublayer(everything, stream, frame_gain, (frame_qkv, frame_out), inner, "frame")

    stream = lax.all_to_all(
        stream.reshape(row_count, col_count, width),
        "view",
        split_axis=0,
        concat_axis=0,
        tiled=True,
        axis_index_groups=spread,
    ).reshape(tokens, width)
    everything = gathered(stream, share, "view", ring)
    copies = sublayer(everything, stream, row1_gain, (row1,), inner, "row1", share)
    everything = lax.all_to_all(
        copies, "view", split_axis=0, concat_axis=0, tiled=True, axis_index_groups=ring
    )
    stream = sublayer(everything, copies[0], row2_gain, (row2,), inner, "row2")
    stream = lax.all_to_all(
        stream.reshape(row_count, col_count, width),
        "view",
        split_axis=0,
        concat_axis=0,
        tiled=True,
        axis_index_groups=spread,
    )
    return stream.reshape(images.shape)


def solution(mesh):
    in_specs = (
        P(("batch", "view"), "band", None, None),
        P(),
        P(),
        P(),
        P(),
        P("band", None),
        P(None, "band"),
        P(),
        P("band", None),
        P(None, "band"),
    )
    out_specs = P(("batch", "view"), "band", None, None)
    return jax.shard_map(local, mesh=mesh, in_specs=in_specs, out_specs=out_specs, check_vma=False)
```

```python
import functools

import jax
import jax.numpy as jnp
from jax import lax
from jax.experimental import pallas as pl
from jax.experimental.pallas import tpu as pltpu
from jax.sharding import PartitionSpec as P


HEAD_DIM = 64
EPSILON = 1e-06
PAIR = 2 * HEAD_DIM


def normed_block(block, gain):
    values = block.astype(jnp.float32)
    factor = lax.rsqrt(jnp.mean(values * values, axis=-1, keepdims=True) + EPSILON)
    return (values * factor * gain).astype(jnp.bfloat16)


def attention_body(transposed_out, all_ref, own_ref, gain_ref, qkv_ref, out_ref, result_ref, kv_ref):
    chunks, tokens, _ = all_ref.shape
    inner = kv_ref.shape[1] // 2
    gain = gain_ref[...]
    for chunk in range(chunks):
        normed = normed_block(all_ref[chunk], gain)
        kv_ref[chunk * tokens : (chunk + 1) * tokens, :] = jnp.dot(
            normed, qkv_ref[:, inner : 3 * inner], preferred_element_type=jnp.float32
        ).astype(jnp.bfloat16)
    own = own_ref[...]
    normed = normed_block(own, gain)
    queries = (
        jnp.dot(normed, qkv_ref[:, :inner], preferred_element_type=jnp.float32)
        .astype(jnp.bfloat16)
    ) * jnp.bfloat16(HEAD_DIM ** (-0.5))
    lane = lax.broadcasted_iota(jnp.int32, (tokens, PAIR), 1)
    first = lane < HEAD_DIM
    attended = []
    for pair in range(inner // PAIR):
        columns = slice(pair * PAIR, (pair + 1) * PAIR)
        query = queries[:, columns]
        keys = kv_ref[:, columns]
        values = kv_ref[:, inner + pair * PAIR : inner + (pair + 1) * PAIR]
        halves = []
        for mask in (first, jnp.logical_not(first)):
            masked = jnp.where(mask, query, jnp.zeros_like(query))
            scores = lax.dot_general(
                masked, keys, (((1,), (1,)), ((), ())), preferred_element_type=jnp.float32
            )
            highest = jnp.max(scores, axis=-1, keepdims=True)
            weights = jnp.exp(scores - highest)
            total = jnp.sum(weights, axis=-1, keepdims=True)
            mixed = jnp.dot(
                weights.astype(jnp.bfloat16), values, preferred_element_type=jnp.float32
            )
            halves.append(mixed / total)
        attended.append(jnp.where(first, halves[0], halves[1]).astype(jnp.bfloat16))
    attended = jnp.concatenate(attended, axis=1)
    contract = (((1,), (1,)), ((), ())) if transposed_out else (((1,), (0,)), ((), ()))
    update = lax.dot_general(
        attended, out_ref[...], contract, preferred_element_type=jnp.float32
    )
    stream = (own.astype(jnp.float32) + update).astype(jnp.bfloat16)
    if len(result_ref.shape) == 2:
        result_ref[...] = stream
    else:
        for copy in range(result_ref.shape[0]):
            result_ref[copy] = stream


def row_body(
    all_ref,
    own_ref,
    gain_ref,
    qkv_ref,
    out_ref,
    one_ref,
    two_ref,
    three_ref,
    other_ref,
    result_ref,
    kv_ref,
    weight_ref,
):
    inner = kv_ref.shape[1] // 2
    pieces, rows, _ = other_ref.shape
    bands = pieces + 1
    band = lax.axis_index("band")
    core = lax.rem(lax.axis_index("batch"), 2)
    start = pl.multiple_of(2 * band * rows, rows)
    weight_ref[pl.ds(start, 2 * rows), : 3 * inner] = qkv_ref[...]
    weight_ref[pl.ds(start, 2 * rows), 3 * inner :] = out_ref[...]
    for index, mine_ref in enumerate((one_ref, two_ref, three_ref)):
        source = lax.rem(band + bands - 1 - index, bands)
        here = pl.multiple_of((2 * source + core) * rows, rows)
        there = pl.multiple_of((2 * source + 1 - core) * rows, rows)
        weight_ref[pl.ds(here, rows), :] = mine_ref[...]
        weight_ref[pl.ds(there, rows), :] = other_ref[index]
    attention_body(
        True,
        all_ref,
        own_ref,
        gain_ref,
        weight_ref.at[:, : 3 * inner],
        weight_ref.at[:, 3 * inner :],
        result_ref,
        kv_ref,
    )


def sublayer(everything, own, gain, weights, inner, copies=None):
    rows = len(weights) > 2
    chunks, tokens, width = everything.shape
    shape = (tokens, width) if copies is None else (copies, tokens, width)
    body = row_body if rows else functools.partial(attention_body, False)
    count = chunks * tokens
    return pl.pallas_call(
        body,
        out_shape=jax.ShapeDtypeStruct(shape, jnp.bfloat16),
        in_specs=[pl.BlockSpec(memory_space=pltpu.VMEM)] * (3 + len(weights)),
        out_specs=pl.BlockSpec(memory_space=pltpu.VMEM),
        scratch_shapes=[pltpu.VMEM((count, 2 * inner), jnp.bfloat16)]
        + [pltpu.VMEM((width, 4 * inner), jnp.bfloat16)] * rows,
        compiler_params=pltpu.CompilerParams(vmem_limit_bytes=12 << 20),
        cost_estimate=pl.CostEstimate(
            flops=2 * count * width * 2 * inner + 4 * tokens * width * inner + 4 * tokens * count * inner,
            bytes_accessed=2 * (count * width + 4 * width * inner),
            transcendentals=tokens * count * inner // HEAD_DIM,
        ),
    )(everything, own, gain, *weights)


def gathered(stream, copies, axis, groups=None):
    return lax.all_to_all(
        jnp.broadcast_to(stream[None], (copies,) + stream.shape),
        axis,
        split_axis=0,
        concat_axis=0,
        tiled=True,
        axis_index_groups=groups,
    )


def layers(
    images,
    frame_gain,
    frame_qkv,
    frame_out,
    row1_gain,
    row1_qkv,
    row1_out,
    row2_gain,
    row2_qkv,
    row2_out,
):
    _, row_count, col_count, width = images.shape
    inner = frame_out.shape[0]
    tokens = row_count * col_count
    views = lax.axis_size("view")
    bands = lax.axis_size("band")
    share = views // row_count
    near = 2
    deep = views // near
    side = share // near
    spread = [
        [y * deep + h * side + l for h in range(row_count)] for y in range(near) for l in range(side)
    ]
    ring = [
        [h * side + l for l in range(side)] + [deep + h * side + l for l in reversed(range(side))]
        for h in range(row_count)
    ]
    siblings = [(i, i ^ 1) for i in range(lax.axis_size("batch"))]
    core = lax.rem(lax.axis_index("batch"), 2)

    def half(qkv, out):
        rows = qkv.shape[0] // 2
        shard = jnp.concatenate([qkv, out.T], axis=1)
        return lax.dynamic_slice(shard, (core * rows, 0), (rows, shard.shape[1]))

    stream = images.reshape(tokens, width)
    everything = lax.all_gather(stream, "band", axis=0, tiled=False)
    stream = sublayer(everything, stream, frame_gain.reshape(1, width), (frame_qkv, frame_out), inner)
    stream, row1_qkv, row1_out, row2_qkv, row2_out = lax.optimization_barrier(
        (stream, row1_qkv, row1_out, row2_qkv, row2_out)
    )

    def pulled(qkv, out):
        piece = half(qkv, out)
        pieces = []
        for step in range(1, bands):
            pieces.append(
                lax.ppermute(piece, "band", [(i, (i + step) % bands) for i in range(bands)])
            )
        return pieces

    gain1 = row1_gain.reshape(1, width)
    gain2 = row2_gain.reshape(1, width)
    mine1 = pulled(row1_qkv, row1_out)
    mine2 = pulled(row2_qkv, row2_out)
    stream = lax.all_to_all(
        stream.reshape(row_count, col_count, width),
        "view",
        split_axis=0,
        concat_axis=0,
        tiled=True,
        axis_index_groups=spread,
    ).reshape(tokens, width)
    other1 = lax.ppermute(jnp.stack(mine1), "batch", siblings)
    other2 = lax.ppermute(jnp.stack(mine2), "batch", siblings)
    everything = gathered(stream, share, "view", ring)
    copies = sublayer(everything, stream, gain1, (row1_qkv, row1_out.T, *mine1, other1), inner, share)
    everything = lax.all_to_all(
        copies, "view", split_axis=0, concat_axis=0, tiled=True, axis_index_groups=ring
    )
    stream = sublayer(everything, copies[0], gain2, (row2_qkv, row2_out.T, *mine2, other2), inner)
    stream = lax.all_to_all(
        stream.reshape(row_count, col_count, width),
        "view",
        split_axis=0,
        concat_axis=0,
        tiled=True,
        axis_index_groups=spread,
    )
    return stream.reshape(images.shape)


def solution(mesh):
    in_specs = (
        P(("batch", "view"), "band", None, None),
        P(),
        P(),
        P(),
        P(),
        P("band", None),
        P(None, "band"),
        P(),
        P("band", None),
        P(None, "band"),
    )
    out_specs = P(("batch", "view"), "band", None, None)
    return jax.shard_map(layers, mesh=mesh, in_specs=in_specs, out_specs=out_specs, check_vma=False)
```

```python
import jax
import jax.numpy as jnp
from jax import lax
from jax.experimental import pallas as pl
from jax.experimental.pallas import tpu as pltpu
from jax.sharding import PartitionSpec as P


HEAD_DIM = 64
EPSILON = 1e-06
PAIR = 2 * HEAD_DIM


def attend(own, all_ref, gain_ref, waits, weight_ref, out_ref, contract, normed_ref, kv_ref, between=None):
    chunks, tokens, width = all_ref.shape
    inner = kv_ref.shape[1] // 2
    gain = gain_ref[...].reshape(1, width)
    for chunk in range(chunks):
        values = all_ref[chunk].astype(jnp.float32)
        factor = lax.rsqrt(jnp.mean(values * values, axis=-1, keepdims=True) + EPSILON)
        normed_ref[chunk * tokens : (chunk + 1) * tokens, :] = (values * factor * gain).astype(
            jnp.bfloat16
        )
    for part in range(2):
        waits[1 + part]()
        for chunk in range(chunks):
            rows = slice(chunk * tokens, (chunk + 1) * tokens)
            kv_ref[rows, part * inner : (part + 1) * inner] = jnp.dot(
                normed_ref[rows, :],
                weight_ref[:, (1 + part) * inner : (2 + part) * inner],
                preferred_element_type=jnp.float32,
            ).astype(jnp.bfloat16)
    waits[0]()
    normed = normed_ref[pl.ds(pl.multiple_of(own * tokens, tokens), tokens), :]
    queries = jnp.dot(
        normed, weight_ref[:, :inner], preferred_element_type=jnp.float32
    ).astype(jnp.bfloat16) * jnp.bfloat16(HEAD_DIM ** (-0.5))
    if between is not None:
        between()
    first = lax.broadcasted_iota(jnp.int32, (tokens, PAIR), 1) < HEAD_DIM
    attended = []
    for pair in range(inner // PAIR):
        columns = slice(pair * PAIR, (pair + 1) * PAIR)
        query = queries[:, columns]
        keys = kv_ref[:, columns]
        values = kv_ref[:, inner + pair * PAIR : inner + (pair + 1) * PAIR]
        halves = []
        for mask in (first, jnp.logical_not(first)):
            scores = lax.dot_general(
                jnp.where(mask, query, jnp.zeros_like(query)),
                keys,
                (((1,), (1,)), ((), ())),
                preferred_element_type=jnp.float32,
            )
            weights = jnp.exp(scores - jnp.max(scores, axis=-1, keepdims=True))
            total = jnp.sum(weights, axis=-1, keepdims=True)
            mixed = jnp.dot(
                weights.astype(jnp.bfloat16), values, preferred_element_type=jnp.float32
            )
            halves.append(mixed / total)
        attended.append(jnp.where(first, halves[0], halves[1]).astype(jnp.bfloat16))
    waits[3]()
    update = lax.dot_general(
        jnp.concatenate(attended, axis=1), out_ref[...], contract, preferred_element_type=jnp.float32
    )
    return (all_ref[own].astype(jnp.float32) + update).astype(jnp.bfloat16)


def started(copies):
    for copy in copies:
        copy.start()

    def wait():
        for copy in copies:
            copy.wait()

    return wait


def frame_body(
    all_ref,
    gain_ref,
    qkv_ref,
    out_ref,
    *refs,
):
    shards, results, scratch = refs[:4], refs[4:9], refs[9:]
    weight_ref, mix_ref, normed_ref, kv_ref, whole_ref, sems = scratch
    inner = kv_ref.shape[1] // 2
    band = lax.axis_index("band")
    core = lax.rem(lax.axis_index("batch"), 2)
    waits = {}
    for order, part in enumerate((1, 2, 0)):
        columns = slice(part * inner, (part + 1) * inner)
        waits[part] = started(
            [pltpu.make_async_copy(qkv_ref.at[:, columns], weight_ref.at[:, columns], sems.at[order])]
        )
    waits[3] = started([pltpu.make_async_copy(out_ref, mix_ref, sems.at[3])])
    loads = [
        started(
            [
                pltpu.make_async_copy(
                    shards[2 * layer], whole_ref.at[layer, :, : 3 * inner], sems.at[4 + 2 * layer]
                ),
                pltpu.make_async_copy(
                    shards[2 * layer + 1], whole_ref.at[layer, :, 3 * inner :], sems.at[5 + 2 * layer]
                ),
            ]
        )
        for layer in range(2)
    ]
    stores = []

    def between():
        for layer, wait in enumerate(loads):
            near, far = results[1 + 2 * layer : 3 + 2 * layer]
            rows = far.shape[0]
            half = pl.ds(pl.multiple_of(core * rows, rows), rows)
            wait()
            stores.append(
                started(
                    [
                        pltpu.make_async_copy(whole_ref.at[layer], near, sems.at[8 + 2 * layer]),
                        pltpu.make_async_copy(whole_ref.at[layer, half, :], far, sems.at[9 + 2 * layer]),
                    ]
                )
            )

    results[0][...] = attend(
        band,
        all_ref,
        gain_ref,
        waits,
        weight_ref,
        mix_ref,
        (((1,), (0,)), ((), ())),
        normed_ref,
        kv_ref,
        between,
    )
    for wait in stores:
        wait()


def kept(*arrays):
    return [pltpu.with_memory_space_constraint(array, pltpu.HBM) for array in arrays]


def frame_layer(everything, gain, qkv, out, shards):
    chunks, tokens, width = everything.shape
    inner = out.shape[0]
    count = chunks * tokens
    rows = shards[0].shape[0]
    near = jax.ShapeDtypeStruct((rows, 4 * inner), jnp.bfloat16)
    far = jax.ShapeDtypeStruct((rows // 2, 4 * inner), jnp.bfloat16)
    vmem = pl.BlockSpec(memory_space=pltpu.VMEM)
    return pl.pallas_call(
        frame_body,
        out_shape=(jax.ShapeDtypeStruct((tokens, width), jnp.bfloat16), near, far, near, far),
        in_specs=[vmem, vmem] + [pl.BlockSpec(memory_space=pltpu.HBM)] * 6,
        out_specs=(vmem,) + (pl.BlockSpec(memory_space=pltpu.HBM),) * 4,
        scratch_shapes=[
            pltpu.VMEM((width, 3 * inner), jnp.bfloat16),
            pltpu.VMEM((inner, width), jnp.bfloat16),
            pltpu.VMEM((count, width), jnp.bfloat16),
            pltpu.VMEM((count, 2 * inner), jnp.bfloat16),
            pltpu.VMEM((2, rows, 4 * inner), jnp.bfloat16),
            pltpu.SemaphoreType.DMA((12,)),
        ],
        compiler_params=pltpu.CompilerParams(vmem_limit_bytes=20 << 20),
        cost_estimate=estimate(chunks, tokens, width, inner),
        name="frame",
    )(everything, gain, *kept(qkv, out, *shards))


def estimate(chunks, tokens, width, inner):
    count = chunks * tokens
    return pl.CostEstimate(
        flops=4 * count * width * inner + 4 * tokens * width * inner + 4 * tokens * count * inner,
        bytes_accessed=2 * (count * width + 4 * width * inner),
        transcendentals=tokens * count * inner // HEAD_DIM,
    )


def row_body(
    all_ref, gain_ref, qkv_ref, out_ref, near_ref, far_ref, other_ref, result_ref, weight_ref, normed_ref, kv_ref, sems
):
    chunks = all_ref.shape[0]
    inner = kv_ref.shape[1] // 2
    rows = far_ref.shape[0]
    bands = lax.axis_size("band")
    band = lax.axis_index("band")
    core = lax.rem(lax.axis_index("batch"), 2)
    view = lax.axis_index("view")
    deep = lax.axis_size("view") // 2
    left = lax.rem(view, 2)
    own = jnp.where(view < deep, left, chunks - 1 - left)

    def place(index, half, count):
        return pl.ds(pl.multiple_of((2 * lax.rem(index, bands) + half) * rows, rows), count)

    down, up = band + bands - 1, band + 1
    target = (
        place(band, 0, 2 * rows),
        place(down + 2 * core, 0, 2 * rows),
        place(band + 2, core, rows),
        place(up + 2 * core, 0, 2 * rows),
        place(band + 2, 1 - core, rows),
    )
    waits = {}
    for order, part in enumerate((1, 2, 0, 3)):
        columns = slice(part * inner, (part + 1) * inner)
        sources = (
            out_ref if part == 3 else qkv_ref.at[:, columns],
            near_ref.at[:, columns],
            far_ref.at[:, columns],
            other_ref.at[: 2 * rows, columns],
            other_ref.at[2 * rows :, columns],
        )
        waits[part] = started(
            [
                pltpu.make_async_copy(source, weight_ref.at[goal, columns], sems.at[order, index])
                for index, (source, goal) in enumerate(zip(sources, target))
            ]
        )
    stream = attend(
        own,
        all_ref,
        gain_ref,
        waits,
        weight_ref,
        weight_ref.at[:, 3 * inner :],
        (((1,), (1,)), ((), ())),
        normed_ref,
        kv_ref,
    )
    if len(result_ref.shape) == 2:
        result_ref[...] = stream
    else:
        for copy in range(result_ref.shape[0]):
            result_ref[copy] = stream


def row_layer(everything, gain, weights, copies=None):
    chunks, tokens, width = everything.shape
    inner = weights[0].shape[1] // 3
    shape = (tokens, width) if copies is None else (copies, tokens, width)
    count = chunks * tokens
    vmem = pl.BlockSpec(memory_space=pltpu.VMEM)
    return pl.pallas_call(
        row_body,
        out_shape=jax.ShapeDtypeStruct(shape, jnp.bfloat16),
        in_specs=[vmem, vmem] + [pl.BlockSpec(memory_space=pltpu.HBM)] * 5,
        out_specs=vmem,
        scratch_shapes=[
            pltpu.VMEM((width, 4 * inner), jnp.bfloat16),
            pltpu.VMEM((count, width), jnp.bfloat16),
            pltpu.VMEM((count, 2 * inner), jnp.bfloat16),
            pltpu.SemaphoreType.DMA((4, 5)),
        ],
        compiler_params=pltpu.CompilerParams(vmem_limit_bytes=20 << 20),
        cost_estimate=estimate(chunks, tokens, width, inner),
    )(everything, gain, *kept(*weights))


def exchanged(stream, rows, groups):
    tokens, width = stream.shape
    return lax.all_to_all(
        stream.reshape(rows, tokens // rows, width),
        "view",
        split_axis=0,
        concat_axis=0,
        tiled=True,
        axis_index_groups=groups,
    ).reshape(tokens, width)


def shared(copies, groups):
    return lax.all_to_all(
        copies, "view", split_axis=0, concat_axis=0, tiled=True, axis_index_groups=groups
    )


def layers(
    images,
    frame_gain,
    frame_qkv,
    frame_out,
    row1_gain,
    row1_qkv,
    row1_out,
    row2_gain,
    row2_qkv,
    row2_out,
):
    _, row_count, col_count, width = images.shape
    tokens = row_count * col_count
    views = lax.axis_size("view")
    bands = lax.axis_size("band")
    batches = lax.axis_size("batch")
    share = views // row_count
    near = 2
    deep = views // near
    side = share // near
    spread = [
        [y * deep + h * side + l for h in range(row_count)] for y in range(near) for l in range(side)
    ]
    ring = [
        [h * side + l for l in range(side)] + [deep + h * side + l for l in reversed(range(side))]
        for h in range(row_count)
    ]
    siblings = [(i, i ^ 1) for i in range(batches)]
    turn = [
        (b * batches + c, ((b + 1 - 2 * (c % 2)) % bands) * batches + c)
        for b in range(bands)
        for c in range(batches)
    ]
    across = [(b, (b + 2) % bands) for b in range(bands)]

    everything = lax.all_gather(images.reshape(tokens, width), "band", axis=0, tiled=False)
    shards = (row1_qkv, row1_out.T, row2_qkv, row2_out.T)
    stream, near1, far1, near2, far2 = frame_layer(
        everything, frame_gain, frame_qkv, frame_out, shards
    )
    stream = exchanged(stream, row_count, spread)
    near1 = lax.ppermute(near1, ("band", "batch"), turn)
    far1 = lax.ppermute(far1, "band", across)
    near2 = lax.ppermute(near2, ("band", "batch"), turn)
    far2 = lax.ppermute(far2, "band", across)
    gain1 = row1_gain.reshape(1, width)
    gain2 = row2_gain.reshape(1, width)
    other1 = lax.ppermute(jnp.concatenate([near1, far1]), "batch", siblings)
    other2 = lax.ppermute(jnp.concatenate([near2, far2]), "batch", siblings)
    everything = shared(jnp.broadcast_to(stream[None], (share, tokens, width)), ring)
    copies = row_layer(everything, gain1, (*shards[:2], near1, far1, other1), share)
    everything = shared(copies, ring)
    stream = row_layer(everything, gain2, (*shards[2:], near2, far2, other2))
    stream = exchanged(stream, row_count, spread)
    return stream.reshape(images.shape)


def solution(mesh):
    in_specs = (
        P(("batch", "view"), "band", None, None),
        P(),
        P(),
        P(),
        P(),
        P("band", None),
        P(None, "band"),
        P(),
        P("band", None),
        P(None, "band"),
    )
    out_specs = P(("batch", "view"), "band", None, None)
    return jax.shard_map(layers, mesh=mesh, in_specs=in_specs, out_specs=out_specs, check_vma=False)
```

```python
import jax
import jax.numpy as jnp
from jax import lax
from jax.experimental import pallas as pl
from jax.experimental.pallas import tpu as pltpu
from jax.sharding import PartitionSpec as P


HEAD_DIM = 64
EPSILON = 1e-06
PAIR = 2 * HEAD_DIM


def project(all_ref, gain_ref, waits, weight_ref, normed_ref, kv_ref):
    chunks, tokens, width = all_ref.shape
    inner = kv_ref.shape[1] // 2
    gain = gain_ref[...].reshape(1, width)
    for chunk in range(chunks):
        values = all_ref[chunk].astype(jnp.float32)
        factor = lax.rsqrt(jnp.mean(values * values, axis=-1, keepdims=True) + EPSILON)
        normed_ref[chunk * tokens : (chunk + 1) * tokens, :] = (values * factor * gain).astype(
            jnp.bfloat16
        )
    for part in range(2):
        waits[1 + part]()
        for chunk in range(chunks):
            rows = slice(chunk * tokens, (chunk + 1) * tokens)
            kv_ref[rows, part * inner : (part + 1) * inner] = jnp.dot(
                normed_ref[rows, :],
                weight_ref[:, (1 + part) * inner : (2 + part) * inner],
                preferred_element_type=jnp.float32,
            ).astype(jnp.bfloat16)
    waits[0]()


def attend(own, all_ref, weight_ref, out_ref, contract, normed_ref, kv_ref):
    _, tokens, _ = all_ref.shape
    inner = kv_ref.shape[1] // 2
    start = own * tokens
    if not isinstance(own, int):
        start = pl.multiple_of(start, tokens)
    queries = jnp.dot(
        normed_ref[pl.ds(start, tokens), :], weight_ref[:, :inner], preferred_element_type=jnp.float32
    ).astype(jnp.bfloat16) * jnp.bfloat16(HEAD_DIM ** (-0.5))
    first = lax.broadcasted_iota(jnp.int32, (tokens, PAIR), 1) < HEAD_DIM
    attended = []
    for pair in range(inner // PAIR):
        columns = slice(pair * PAIR, (pair + 1) * PAIR)
        query = queries[:, columns]
        keys = kv_ref[:, columns]
        values = kv_ref[:, inner + pair * PAIR : inner + (pair + 1) * PAIR]
        halves = []
        for mask in (first, jnp.logical_not(first)):
            scores = lax.dot_general(
                jnp.where(mask, query, jnp.zeros_like(query)),
                keys,
                (((1,), (1,)), ((), ())),
                preferred_element_type=jnp.float32,
            )
            weights = jnp.exp(scores - jnp.max(scores, axis=-1, keepdims=True))
            total = jnp.sum(weights, axis=-1, keepdims=True)
            mixed = jnp.dot(
                weights.astype(jnp.bfloat16), values, preferred_element_type=jnp.float32
            )
            halves.append(mixed / total)
        attended.append(jnp.where(first, halves[0], halves[1]).astype(jnp.bfloat16))
    update = lax.dot_general(
        jnp.concatenate(attended, axis=1), out_ref[...], contract, preferred_element_type=jnp.float32
    )
    return (all_ref[own].astype(jnp.float32) + update).astype(jnp.bfloat16)


def started(copies):
    for copy in copies:
        copy.start()

    def wait():
        for copy in copies:
            copy.wait()

    return wait


def packing(qkv, out, near, far, whole, sems, core):
    columns = qkv.shape[1]
    rows = far.shape[0]
    half = pl.ds(pl.multiple_of(core * rows, rows), rows)
    load = started(
        [
            pltpu.make_async_copy(qkv, whole.at[:, :columns], sems.at[0]),
            pltpu.make_async_copy(out, whole.at[:, columns:], sems.at[1]),
        ]
    )

    def store():
        load()
        return started(
            [
                pltpu.make_async_copy(whole, near, sems.at[2]),
                pltpu.make_async_copy(whole.at[half, :], far, sems.at[3]),
            ]
        )

    return store


def pack_body(qkv_ref, out_ref, near_ref, far_ref, whole_ref, sems):
    core = lax.rem(lax.axis_index("batch"), 2)
    packing(qkv_ref, out_ref, near_ref, far_ref, whole_ref, sems, core)()()


def pack_layer(qkv, out):
    rows, columns = qkv.shape[0], qkv.shape[1] + out.shape[1]
    hbm = pl.BlockSpec(memory_space=pltpu.HBM)
    return pl.pallas_call(
        pack_body,
        out_shape=(
            jax.ShapeDtypeStruct((rows, columns), jnp.bfloat16),
            jax.ShapeDtypeStruct((rows // 2, columns), jnp.bfloat16),
        ),
        in_specs=[hbm, hbm],
        out_specs=(hbm, hbm),
        scratch_shapes=[pltpu.VMEM((rows, columns), jnp.bfloat16), pltpu.SemaphoreType.DMA((4,))],
        compiler_params=pltpu.CompilerParams(vmem_limit_bytes=4 << 20),
        name="pack",
    )(*kept(qkv, out))


def frame_body(
    all_ref,
    gain_ref,
    qkv_ref,
    out_ref,
    row_qkv_ref,
    row_out_ref,
    result_ref,
    near_ref,
    far_ref,
    weight_ref,
    mix_ref,
    normed_ref,
    kv_ref,
    whole_ref,
    sems,
    pack_sems,
):
    inner = kv_ref.shape[1] // 2
    band = lax.axis_index("band")
    core = lax.rem(lax.axis_index("batch"), 2)
    waits = {}
    for order, part in enumerate((1, 2, 0)):
        columns = slice(part * inner, (part + 1) * inner)
        waits[part] = started(
            [pltpu.make_async_copy(qkv_ref.at[:, columns], weight_ref.at[:, columns], sems.at[order])]
        )
    mix = started([pltpu.make_async_copy(out_ref, mix_ref, sems.at[3])])
    store = packing(row_qkv_ref, row_out_ref, near_ref, far_ref, whole_ref, pack_sems, core)
    project(all_ref, gain_ref, waits, weight_ref, normed_ref, kv_ref)
    mix()
    stored = store()
    result_ref[...] = attend(
        band, all_ref, weight_ref, mix_ref, (((1,), (0,)), ((), ())), normed_ref, kv_ref
    )
    stored()


def kept(*arrays):
    return [pltpu.with_memory_space_constraint(array, pltpu.HBM) for array in arrays]


def frame_layer(everything, gain, qkv, out, row_qkv, row_out):
    chunks, tokens, width = everything.shape
    inner = out.shape[0]
    count = chunks * tokens
    rows = row_qkv.shape[0]
    vmem = pl.BlockSpec(memory_space=pltpu.VMEM)
    hbm = pl.BlockSpec(memory_space=pltpu.HBM)
    return pl.pallas_call(
        frame_body,
        out_shape=(
            jax.ShapeDtypeStruct((tokens, width), jnp.bfloat16),
            jax.ShapeDtypeStruct((rows, 4 * inner), jnp.bfloat16),
            jax.ShapeDtypeStruct((rows // 2, 4 * inner), jnp.bfloat16),
        ),
        in_specs=[vmem, vmem] + [hbm] * 4,
        out_specs=(vmem, hbm, hbm),
        scratch_shapes=[
            pltpu.VMEM((width, 3 * inner), jnp.bfloat16),
            pltpu.VMEM((inner, width), jnp.bfloat16),
            pltpu.VMEM((count, width), jnp.bfloat16),
            pltpu.VMEM((count, 2 * inner), jnp.bfloat16),
            pltpu.VMEM((rows, 4 * inner), jnp.bfloat16),
            pltpu.SemaphoreType.DMA((4,)),
            pltpu.SemaphoreType.DMA((4,)),
        ],
        compiler_params=pltpu.CompilerParams(vmem_limit_bytes=20 << 20),
        cost_estimate=estimate(chunks, tokens, width, inner),
        name="frame",
    )(everything, gain, *kept(qkv, out, row_qkv, row_out))


def estimate(chunks, tokens, width, inner):
    count = chunks * tokens
    return pl.CostEstimate(
        flops=4 * count * width * inner + 4 * tokens * width * inner + 4 * tokens * count * inner,
        bytes_accessed=2 * (count * width + 4 * width * inner),
        transcendentals=tokens * count * inner // HEAD_DIM,
    )


def assembled(parts, weight_ref, sems, band, bands, core):
    qkv_ref, out_ref, near_ref, far_ref, other_ref = parts
    inner = out_ref.shape[1]
    rows = far_ref.shape[0]

    def place(index, half, count):
        return pl.ds(pl.multiple_of((2 * lax.rem(index, bands) + half) * rows, rows), count)

    down, up = band + bands - 1, band + 1
    target = (
        place(band, 0, 2 * rows),
        place(down + 2 * core, 0, 2 * rows),
        place(band + 2, core, rows),
        place(up + 2 * core, 0, 2 * rows),
        place(band + 2, 1 - core, rows),
    )
    waits = {}
    for order, part in enumerate((1, 2, 0, 3)):
        columns = slice(part * inner, (part + 1) * inner)
        sources = (
            out_ref if part == 3 else qkv_ref.at[:, columns],
            near_ref.at[:, columns],
            far_ref.at[:, columns],
            other_ref.at[: 2 * rows, columns],
            other_ref.at[2 * rows :, columns],
        )
        waits[part] = started(
            [
                pltpu.make_async_copy(source, weight_ref.at[goal, columns], sems.at[order, index])
                for index, (source, goal) in enumerate(zip(sources, target))
            ]
        )
    return waits


def rows_body(all_ref, gain1_ref, gain2_ref, *refs):
    parts1, parts2 = refs[:5], refs[5:10]
    result_ref, weight1_ref, weight2_ref, normed_ref, kv_ref, stream_ref, sems = refs[10:]
    chunks = all_ref.shape[0]
    inner = kv_ref.shape[1] // 2
    bands = lax.axis_size("band")
    band = lax.axis_index("band")
    core = lax.rem(lax.axis_index("batch"), 2)
    view = lax.axis_index("view")
    deep = lax.axis_size("view") // 2
    left = lax.rem(view, 2)
    own = jnp.where(view < deep, left, chunks - 1 - left)
    contract = (((1,), (1,)), ((), ()))
    waits1 = assembled(parts1, weight1_ref, sems.at[0], band, bands, core)
    waits2 = assembled(parts2, weight2_ref, sems.at[1], band, bands, core)
    project(all_ref, gain1_ref, waits1, weight1_ref, normed_ref, kv_ref)
    waits1[3]()

    @pl.loop(0, chunks)
    def _(chunk):
        stream_ref[chunk] = attend(
            chunk, all_ref, weight1_ref, weight1_ref.at[:, 3 * inner :], contract, normed_ref, kv_ref
        )

    project(stream_ref, gain2_ref, waits2, weight2_ref, normed_ref, kv_ref)
    waits2[3]()
    result_ref[...] = attend(
        own, stream_ref, weight2_ref, weight2_ref.at[:, 3 * inner :], contract, normed_ref, kv_ref
    )


def rows_layer(everything, gain1, gain2, weights1, weights2):
    chunks, tokens, width = everything.shape
    inner = weights1[1].shape[1]
    count = chunks * tokens
    vmem = pl.BlockSpec(memory_space=pltpu.VMEM)
    return pl.pallas_call(
        rows_body,
        out_shape=jax.ShapeDtypeStruct((tokens, width), jnp.bfloat16),
        in_specs=[vmem] * 3 + [pl.BlockSpec(memory_space=pltpu.HBM)] * 10,
        out_specs=vmem,
        scratch_shapes=[
            pltpu.VMEM((width, 4 * inner), jnp.bfloat16),
            pltpu.VMEM((width, 4 * inner), jnp.bfloat16),
            pltpu.VMEM((count, width), jnp.bfloat16),
            pltpu.VMEM((count, 2 * inner), jnp.bfloat16),
            pltpu.VMEM((chunks, tokens, width), jnp.bfloat16),
            pltpu.SemaphoreType.DMA((2, 4, 5)),
        ],
        compiler_params=pltpu.CompilerParams(vmem_limit_bytes=24 << 20),
        cost_estimate=estimate(chunks, tokens, width, inner),
        name="rows",
    )(everything, gain1, gain2, *kept(*weights1, *weights2))


def exchanged(stream, rows, groups):
    tokens, width = stream.shape
    return lax.all_to_all(
        stream.reshape(rows, tokens // rows, width),
        "view",
        split_axis=0,
        concat_axis=0,
        tiled=True,
        axis_index_groups=groups,
    ).reshape(tokens, width)


def shared(copies, groups):
    return lax.all_to_all(
        copies, "view", split_axis=0, concat_axis=0, tiled=True, axis_index_groups=groups
    )


def layers(
    images,
    frame_gain,
    frame_qkv,
    frame_out,
    row1_gain,
    row1_qkv,
    row1_out,
    row2_gain,
    row2_qkv,
    row2_out,
):
    _, row_count, col_count, width = images.shape
    tokens = row_count * col_count
    views = lax.axis_size("view")
    bands = lax.axis_size("band")
    batches = lax.axis_size("batch")
    share = views // row_count
    near = 2
    deep = views // near
    side = share // near
    spread = [
        [y * deep + h * side + l for h in range(row_count)] for y in range(near) for l in range(side)
    ]
    ring = [
        [h * side + l for l in range(side)] + [deep + h * side + l for l in reversed(range(side))]
        for h in range(row_count)
    ]
    siblings = [(i, i ^ 1) for i in range(batches)]
    turn = [
        (b * batches + c, ((b + 1 - 2 * (c % 2)) % bands) * batches + c)
        for b in range(bands)
        for c in range(batches)
    ]
    across = [(b, (b + 2) % bands) for b in range(bands)]

    shards = (row1_qkv, row1_out.T, row2_qkv, row2_out.T)
    near1, far1 = pack_layer(*shards[:2])
    everything = lax.all_gather(images.reshape(tokens, width), "band", axis=0, tiled=False)
    everything, near1, far1 = lax.optimization_barrier((everything, near1, far1))
    near1 = lax.ppermute(near1, ("band", "batch"), turn)
    far1 = lax.ppermute(far1, "band", across)
    stream, near2, far2 = frame_layer(everything, frame_gain, frame_qkv, frame_out, *shards[2:])
    stream = exchanged(stream, row_count, spread)
    near2 = lax.ppermute(near2, ("band", "batch"), turn)
    far2 = lax.ppermute(far2, "band", across)
    other1 = lax.ppermute(jnp.concatenate([near1, far1]), "batch", siblings)
    gain1 = row1_gain.reshape(1, width)
    gain2 = row2_gain.reshape(1, width)
    everything = shared(jnp.broadcast_to(stream[None], (share, tokens, width)), ring)
    other2 = lax.ppermute(jnp.concatenate([near2, far2]), "batch", siblings)
    stream = rows_layer(
        everything,
        gain1,
        gain2,
        (*shards[:2], near1, far1, other1),
        (*shards[2:], near2, far2, other2),
    )
    stream = exchanged(stream, row_count, spread)
    return stream.reshape(images.shape)


def solution(mesh):
    in_specs = (
        P(("batch", "view"), "band", None, None),
        P(),
        P(),
        P(),
        P(),
        P("band", None),
        P(None, "band"),
        P(),
        P("band", None),
        P(None, "band"),
    )
    out_specs = P(("batch", "view"), "band", None, None)
    return jax.shard_map(layers, mesh=mesh, in_specs=in_specs, out_specs=out_specs, check_vma=False)
```

```python
import math

import jax
import jax.numpy as jnp
from jax import lax
from jax.experimental import pallas as pl
from jax.experimental.pallas import tpu as pltpu
from jax.sharding import PartitionSpec as P


HEAD_DIM = 64
EPSILON = 1e-06
PAIR = 2 * HEAD_DIM
SCALE = HEAD_DIM ** (-0.5) * math.log2(math.e)
NORM_ROWS = 32
SOFTMAX_ROWS = 32


def project(all_ref, gain_ref, waits, weight_ref, normed_ref, kv_ref):
    chunks, tokens, width = all_ref.shape
    inner = kv_ref.shape[1] // 2
    gain = gain_ref[...].reshape(1, width)
    for chunk in range(chunks):
        for start in range(0, tokens, NORM_ROWS):
            values = all_ref[chunk, start : start + NORM_ROWS].astype(jnp.float32)
            factor = lax.rsqrt(jnp.mean(values * values, axis=-1, keepdims=True) + EPSILON)
            at = chunk * tokens + start
            normed_ref[at : at + NORM_ROWS, :] = (values * factor * gain).astype(jnp.bfloat16)
    for part in range(2):
        waits[1 + part]()
        kv_ref[:, part * inner : (part + 1) * inner] = jnp.dot(
            normed_ref[...],
            weight_ref[:, (1 + part) * inner : (2 + part) * inner],
            preferred_element_type=jnp.float32,
        ).astype(jnp.bfloat16)
    waits[0]()


def mixed(normed, weight_ref, kv_ref, query_ref, score_ref, rounded_ref, inverse_ref, attended_ref):
    count = normed.shape[0]
    inner = kv_ref.shape[1] // 2
    queries = (
        jnp.dot(normed, weight_ref[:, :inner], preferred_element_type=jnp.float32) * SCALE
    ).astype(jnp.bfloat16)
    first = lax.broadcasted_iota(jnp.int32, (count, PAIR), 1) < HEAD_DIM
    zeros = jnp.zeros((count, PAIR), jnp.bfloat16)
    for pair in range(inner // PAIR):
        query = queries[:, pair * PAIR : (pair + 1) * PAIR]
        query_ref[pair, :count] = jnp.where(first, query, zeros)
        query_ref[pair, count:] = jnp.where(first, zeros, query)
    for pair in range(inner // PAIR):
        slot = pair % 2
        columns = slice(pair * PAIR, (pair + 1) * PAIR)
        score_ref[slot] = lax.dot_general(
            query_ref[pair],
            kv_ref[:, columns],
            (((1,), (1,)), ((), ())),
            preferred_element_type=jnp.float32,
        )
        for start in range(0, 2 * count, SOFTMAX_ROWS):
            rows = slice(start, start + SOFTMAX_ROWS)
            scores = score_ref[slot, rows]
            weights = jnp.exp2(scores - jnp.max(scores, axis=-1, keepdims=True))
            total = jnp.sum(weights, axis=-1, keepdims=True)
            rounded_ref[slot, rows] = weights.astype(jnp.bfloat16)
            inverse_ref[slot, rows] = jnp.broadcast_to(1.0 / total, (SOFTMAX_ROWS, PAIR))
        result = inverse_ref[slot] * jnp.dot(
            rounded_ref[slot],
            kv_ref[:, inner + pair * PAIR : inner + (pair + 1) * PAIR],
            preferred_element_type=jnp.float32,
        )
        attended_ref[:, columns] = jnp.where(first, result[:count], result[count:]).astype(
            jnp.bfloat16
        )


def mixing_scratch(count, keys, inner):
    pairs = inner // PAIR
    return [
        pltpu.VMEM((pairs, 2 * count, PAIR), jnp.bfloat16),
        pltpu.VMEM((2, 2 * count, keys), jnp.float32),
        pltpu.VMEM((2, 2 * count, keys), jnp.bfloat16),
        pltpu.VMEM((2, 2 * count, PAIR), jnp.float32),
        pltpu.VMEM((count, inner), jnp.bfloat16),
    ]


def chunk_of(normed_ref, own, tokens):
    return normed_ref[pl.ds(pl.multiple_of(own * tokens, tokens), tokens), :]


def started(copies):
    for copy in copies:
        copy.start()

    def wait():
        for copy in copies:
            copy.wait()

    return wait


def packing(qkv, out, near, far, whole, sems, core):
    columns = qkv.shape[1]
    rows = far.shape[0]
    half = pl.ds(pl.multiple_of(core * rows, rows), rows)
    load = started(
        [
            pltpu.make_async_copy(qkv, whole.at[:, :columns], sems.at[0]),
            pltpu.make_async_copy(out, whole.at[:, columns:], sems.at[1]),
        ]
    )

    def store():
        load()
        return started(
            [
                pltpu.make_async_copy(whole, near, sems.at[2]),
                pltpu.make_async_copy(whole.at[half, :], far, sems.at[3]),
            ]
        )

    return store


def pack_body(qkv_ref, out_ref, near_ref, far_ref, whole_ref, sems):
    core = lax.rem(lax.axis_index("batch"), 2)
    packing(qkv_ref, out_ref, near_ref, far_ref, whole_ref, sems, core)()()


def pack_layer(qkv, out):
    rows, columns = qkv.shape[0], qkv.shape[1] + out.shape[1]
    hbm = pl.BlockSpec(memory_space=pltpu.HBM)
    return pl.pallas_call(
        pack_body,
        out_shape=(
            jax.ShapeDtypeStruct((rows, columns), jnp.bfloat16),
            jax.ShapeDtypeStruct((rows // 2, columns), jnp.bfloat16),
        ),
        in_specs=[hbm, hbm],
        out_specs=(hbm, hbm),
        scratch_shapes=[pltpu.VMEM((rows, columns), jnp.bfloat16), pltpu.SemaphoreType.DMA((4,))],
        compiler_params=pltpu.CompilerParams(vmem_limit_bytes=4 << 20),
        name="pack",
    )(*kept(qkv, out))


def frame_body(
    all_ref,
    gain_ref,
    qkv_ref,
    out_ref,
    row_qkv_ref,
    row_out_ref,
    result_ref,
    near_ref,
    far_ref,
    weight_ref,
    mix_ref,
    normed_ref,
    kv_ref,
    whole_ref,
    sems,
    pack_sems,
    *mixing,
):
    inner = kv_ref.shape[1] // 2
    band = lax.axis_index("band")
    core = lax.rem(lax.axis_index("batch"), 2)
    waits = {}
    for order, part in enumerate((1, 2, 0)):
        columns = slice(part * inner, (part + 1) * inner)
        waits[part] = started(
            [pltpu.make_async_copy(qkv_ref.at[:, columns], weight_ref.at[:, columns], sems.at[order])]
        )
    mix = started([pltpu.make_async_copy(out_ref, mix_ref, sems.at[3])])
    store = packing(row_qkv_ref, row_out_ref, near_ref, far_ref, whole_ref, pack_sems, core)
    project(all_ref, gain_ref, waits, weight_ref, normed_ref, kv_ref)
    mix()
    stored = store()
    _, tokens, _ = all_ref.shape
    mixed(chunk_of(normed_ref, band, tokens), weight_ref, kv_ref, *mixing)
    update = jnp.dot(mixing[-1][...], mix_ref[...], preferred_element_type=jnp.float32)
    result_ref[...] = (all_ref[band].astype(jnp.float32) + update).astype(jnp.bfloat16)
    stored()


def kept(*arrays):
    return [pltpu.with_memory_space_constraint(array, pltpu.HBM) for array in arrays]


def frame_layer(everything, gain, qkv, out, row_qkv, row_out):
    chunks, tokens, width = everything.shape
    inner = out.shape[0]
    count = chunks * tokens
    rows = row_qkv.shape[0]
    vmem = pl.BlockSpec(memory_space=pltpu.VMEM)
    hbm = pl.BlockSpec(memory_space=pltpu.HBM)
    return pl.pallas_call(
        frame_body,
        out_shape=(
            jax.ShapeDtypeStruct((tokens, width), jnp.bfloat16),
            jax.ShapeDtypeStruct((rows, 4 * inner), jnp.bfloat16),
            jax.ShapeDtypeStruct((rows // 2, 4 * inner), jnp.bfloat16),
        ),
        in_specs=[vmem, vmem] + [hbm] * 4,
        out_specs=(vmem, hbm, hbm),
        scratch_shapes=[
            pltpu.VMEM((width, 3 * inner), jnp.bfloat16),
            pltpu.VMEM((inner, width), jnp.bfloat16),
            pltpu.VMEM((count, width), jnp.bfloat16),
            pltpu.VMEM((count, 2 * inner), jnp.bfloat16),
            pltpu.VMEM((rows, 4 * inner), jnp.bfloat16),
            pltpu.SemaphoreType.DMA((4,)),
            pltpu.SemaphoreType.DMA((4,)),
        ]
        + mixing_scratch(tokens, count, inner),
        compiler_params=pltpu.CompilerParams(vmem_limit_bytes=20 << 20),
        cost_estimate=estimate(chunks, tokens, width, inner),
        name="frame",
    )(everything, gain, *kept(qkv, out, row_qkv, row_out))


def estimate(chunks, tokens, width, inner):
    count = chunks * tokens
    return pl.CostEstimate(
        flops=4 * count * width * inner + 4 * tokens * width * inner + 4 * tokens * count * inner,
        bytes_accessed=2 * (count * width + 4 * width * inner),
        transcendentals=tokens * count * inner // HEAD_DIM,
    )


def assembled(parts, weight_ref, sems, band, bands, core):
    qkv_ref, out_ref, near_ref, far_ref, other_ref = parts
    inner = out_ref.shape[1]
    rows = far_ref.shape[0]

    def place(index, half, count):
        return pl.ds(pl.multiple_of((2 * lax.rem(index, bands) + half) * rows, rows), count)

    down, up = band + bands - 1, band + 1
    target = (
        place(band, 0, 2 * rows),
        place(down + 2 * core, 0, 2 * rows),
        place(band + 2, core, rows),
        place(up + 2 * core, 0, 2 * rows),
        place(band + 2, 1 - core, rows),
    )
    waits = {}
    for order, part in enumerate((1, 2, 0, 3)):
        columns = slice(part * inner, (part + 1) * inner)
        sources = (
            out_ref if part == 3 else qkv_ref.at[:, columns],
            near_ref.at[:, columns],
            far_ref.at[:, columns],
            other_ref.at[: 2 * rows, columns],
            other_ref.at[2 * rows :, columns],
        )
        waits[part] = started(
            [
                pltpu.make_async_copy(source, weight_ref.at[goal, columns], sems.at[order, index])
                for index, (source, goal) in enumerate(zip(sources, target))
            ]
        )
    return waits


def rows_body(all_ref, gain1_ref, gain2_ref, *refs):
    parts1, parts2 = refs[:5], refs[5:10]
    result_ref, weight1_ref, weight2_ref, normed_ref, kv_ref, stream_ref, sems = refs[10:17]
    mixing1, mixing2 = refs[17:22], refs[22:]
    chunks = all_ref.shape[0]
    inner = kv_ref.shape[1] // 2
    bands = lax.axis_size("band")
    band = lax.axis_index("band")
    core = lax.rem(lax.axis_index("batch"), 2)
    view = lax.axis_index("view")
    deep = lax.axis_size("view") // 2
    left = lax.rem(view, 2)
    own = jnp.where(view < deep, left, chunks - 1 - left)
    contract = (((1,), (1,)), ((), ()))
    waits1 = assembled(parts1, weight1_ref, sems.at[0], band, bands, core)
    waits2 = assembled(parts2, weight2_ref, sems.at[1], band, bands, core)
    project(all_ref, gain1_ref, waits1, weight1_ref, normed_ref, kv_ref)
    _, tokens, _ = all_ref.shape
    mixed(normed_ref[...], weight1_ref, kv_ref, *mixing1)
    waits1[3]()
    update = lax.dot_general(
        mixing1[-1][...], weight1_ref[:, 3 * inner :], contract, preferred_element_type=jnp.float32
    )
    for chunk in range(chunks):
        stream_ref[chunk] = (
            all_ref[chunk].astype(jnp.float32) + update[chunk * tokens : (chunk + 1) * tokens]
        ).astype(jnp.bfloat16)
    project(stream_ref, gain2_ref, waits2, weight2_ref, normed_ref, kv_ref)
    mixed(chunk_of(normed_ref, own, tokens), weight2_ref, kv_ref, *mixing2)
    waits2[3]()
    update = lax.dot_general(
        mixing2[-1][...], weight2_ref[:, 3 * inner :], contract, preferred_element_type=jnp.float32
    )
    result_ref[...] = (stream_ref[own].astype(jnp.float32) + update).astype(jnp.bfloat16)


def rows_layer(everything, gain1, gain2, weights1, weights2):
    chunks, tokens, width = everything.shape
    inner = weights1[1].shape[1]
    count = chunks * tokens
    vmem = pl.BlockSpec(memory_space=pltpu.VMEM)
    return pl.pallas_call(
        rows_body,
        out_shape=jax.ShapeDtypeStruct((tokens, width), jnp.bfloat16),
        in_specs=[vmem] * 3 + [pl.BlockSpec(memory_space=pltpu.HBM)] * 10,
        out_specs=vmem,
        scratch_shapes=[
            pltpu.VMEM((width, 4 * inner), jnp.bfloat16),
            pltpu.VMEM((width, 4 * inner), jnp.bfloat16),
            pltpu.VMEM((count, width), jnp.bfloat16),
            pltpu.VMEM((count, 2 * inner), jnp.bfloat16),
            pltpu.VMEM((chunks, tokens, width), jnp.bfloat16),
            pltpu.SemaphoreType.DMA((2, 4, 5)),
        ]
        + mixing_scratch(count, count, inner)
        + mixing_scratch(tokens, count, inner),
        compiler_params=pltpu.CompilerParams(vmem_limit_bytes=32 << 20),
        cost_estimate=estimate(chunks, tokens, width, inner),
        name="rows",
    )(everything, gain1, gain2, *kept(*weights1, *weights2))


def exchanged(stream, rows, groups):
    tokens, width = stream.shape
    return lax.all_to_all(
        stream.reshape(rows, tokens // rows, width),
        "view",
        split_axis=0,
        concat_axis=0,
        tiled=True,
        axis_index_groups=groups,
    ).reshape(tokens, width)


def shared(copies, groups):
    return lax.all_to_all(
        copies, "view", split_axis=0, concat_axis=0, tiled=True, axis_index_groups=groups
    )


def layers(
    images,
    frame_gain,
    frame_qkv,
    frame_out,
    row1_gain,
    row1_qkv,
    row1_out,
    row2_gain,
    row2_qkv,
    row2_out,
):
    _, row_count, col_count, width = images.shape
    tokens = row_count * col_count
    views = lax.axis_size("view")
    bands = lax.axis_size("band")
    batches = lax.axis_size("batch")
    share = views // row_count
    near = 2
    deep = views // near
    side = share // near
    spread = [
        [y * deep + h * side + l for h in range(row_count)] for y in range(near) for l in range(side)
    ]
    ring = [
        [h * side + l for l in range(side)] + [deep + h * side + l for l in reversed(range(side))]
        for h in range(row_count)
    ]
    siblings = [(i, i ^ 1) for i in range(batches)]
    turn = [
        (b * batches + c, ((b + 1 - 2 * (c % 2)) % bands) * batches + c)
        for b in range(bands)
        for c in range(batches)
    ]
    across = [(b, (b + 2) % bands) for b in range(bands)]

    shards = (row1_qkv, row1_out.T, row2_qkv, row2_out.T)
    near1, far1 = pack_layer(*shards[:2])
    everything = lax.all_gather(images.reshape(tokens, width), "band", axis=0, tiled=False)
    everything, near1, far1 = lax.optimization_barrier((everything, near1, far1))
    near1 = lax.ppermute(near1, ("band", "batch"), turn)
    far1 = lax.ppermute(far1, "band", across)
    stream, near2, far2 = frame_layer(everything, frame_gain, frame_qkv, frame_out, *shards[2:])
    stream = exchanged(stream, row_count, spread)
    near2 = lax.ppermute(near2, ("band", "batch"), turn)
    far2 = lax.ppermute(far2, "band", across)
    other1 = lax.ppermute(jnp.concatenate([near1, far1]), "batch", siblings)
    gain1 = row1_gain.reshape(1, width)
    gain2 = row2_gain.reshape(1, width)
    everything = shared(jnp.broadcast_to(stream[None], (share, tokens, width)), ring)
    other2 = lax.ppermute(jnp.concatenate([near2, far2]), "batch", siblings)
    stream = rows_layer(
        everything,
        gain1,
        gain2,
        (*shards[:2], near1, far1, other1),
        (*shards[2:], near2, far2, other2),
    )
    stream = exchanged(stream, row_count, spread)
    return stream.reshape(images.shape)


def solution(mesh):
    in_specs = (
        P(("batch", "view"), "band", None, None),
        P(),
        P(),
        P(),
        P(),
        P("band", None),
        P(None, "band"),
        P(),
        P("band", None),
        P(None, "band"),
    )
    out_specs = P(("batch", "view"), "band", None, None)
    return jax.shard_map(layers, mesh=mesh, in_specs=in_specs, out_specs=out_specs, check_vma=False)
```

```python
import math

import jax
import jax.numpy as jnp
from jax import lax
from jax.experimental import pallas as pl
from jax.experimental.pallas import tpu as pltpu
from jax.sharding import PartitionSpec as P


HEAD_DIM = 64
EPSILON = 1e-06
PAIR = 2 * HEAD_DIM
SCALE = HEAD_DIM ** (-0.5) * math.log2(math.e)
NORM_ROWS = 32
SOFTMAX_ROWS = 32


def project(all_ref, gain_ref, waits, weight_ref, normed_ref, kv_ref):
    chunks, tokens, width = all_ref.shape
    inner = kv_ref.shape[1] // 2
    gain = gain_ref[...].reshape(1, width)
    for chunk in range(chunks):
        for start in range(0, tokens, NORM_ROWS):
            values = all_ref[chunk, start : start + NORM_ROWS].astype(jnp.float32)
            factor = lax.rsqrt(jnp.mean(values * values, axis=-1, keepdims=True) + EPSILON)
            at = chunk * tokens + start
            normed_ref[at : at + NORM_ROWS, :] = (values * factor * gain).astype(jnp.bfloat16)
    for part in range(2):
        waits[1 + part]()
        kv_ref[:, part * inner : (part + 1) * inner] = jnp.dot(
            normed_ref[...],
            weight_ref[:, (1 + part) * inner : (2 + part) * inner],
            preferred_element_type=jnp.float32,
        ).astype(jnp.bfloat16)
    waits[0]()


def mixed(normed, weight_ref, kv_ref, query_ref, score_ref, rounded_ref, inverse_ref, attended_ref):
    count = normed.shape[0]
    inner = kv_ref.shape[1] // 2
    queries = (
        jnp.dot(normed, weight_ref[:, :inner], preferred_element_type=jnp.float32) * SCALE
    ).astype(jnp.bfloat16)
    first = lax.broadcasted_iota(jnp.int32, (count, PAIR), 1) < HEAD_DIM
    zeros = jnp.zeros((count, PAIR), jnp.bfloat16)
    for pair in range(inner // PAIR):
        query = queries[:, pair * PAIR : (pair + 1) * PAIR]
        query_ref[pair, :count] = jnp.where(first, query, zeros)
        query_ref[pair, count:] = jnp.where(first, zeros, query)
    for pair in range(inner // PAIR):
        slot = pair % 2
        columns = slice(pair * PAIR, (pair + 1) * PAIR)
        score_ref[slot] = lax.dot_general(
            query_ref[pair],
            kv_ref[:, columns],
            (((1,), (1,)), ((), ())),
            preferred_element_type=jnp.float32,
        )
        for start in range(0, 2 * count, SOFTMAX_ROWS):
            rows = slice(start, start + SOFTMAX_ROWS)
            scores = score_ref[slot, rows]
            weights = jnp.exp2(scores - jnp.max(scores, axis=-1, keepdims=True))
            total = jnp.sum(weights, axis=-1, keepdims=True)
            rounded_ref[slot, rows] = weights.astype(jnp.bfloat16)
            inverse_ref[slot, rows] = jnp.broadcast_to(1.0 / total, (SOFTMAX_ROWS, PAIR))
        result = inverse_ref[slot] * jnp.dot(
            rounded_ref[slot],
            kv_ref[:, inner + pair * PAIR : inner + (pair + 1) * PAIR],
            preferred_element_type=jnp.float32,
        )
        attended_ref[:, columns] = jnp.where(first, result[:count], result[count:]).astype(
            jnp.bfloat16
        )


def mixing_scratch(count, keys, inner):
    pairs = inner // PAIR
    return [
        pltpu.VMEM((pairs, 2 * count, PAIR), jnp.bfloat16),
        pltpu.VMEM((2, 2 * count, keys), jnp.float32),
        pltpu.VMEM((2, 2 * count, keys), jnp.bfloat16),
        pltpu.VMEM((2, 2 * count, PAIR), jnp.float32),
        pltpu.VMEM((count, inner), jnp.bfloat16),
    ]


def chunk_of(normed_ref, own, tokens):
    return normed_ref[pl.ds(pl.multiple_of(own * tokens, tokens), tokens), :]


def started(copies):
    for copy in copies:
        copy.start()

    def wait():
        for copy in copies:
            copy.wait()

    return wait


def pack_body(*refs):
    shards, near_ref, sems = refs[:4], refs[4], refs[5]
    columns = shards[0].shape[1]
    copies = []
    for layer in range(2):
        qkv, out = shards[2 * layer : 2 * layer + 2]
        copies.append(
            pltpu.make_async_copy(qkv, near_ref.at[layer, :, :columns], sems.at[2 * layer])
        )
        copies.append(
            pltpu.make_async_copy(out, near_ref.at[layer, :, columns:], sems.at[2 * layer + 1])
        )
    started(copies)()


def pack_layer(shards):
    qkv, out = shards[:2]
    return pl.pallas_call(
        pack_body,
        out_shape=jax.ShapeDtypeStruct((2, qkv.shape[0], qkv.shape[1] + out.shape[1]), jnp.bfloat16),
        in_specs=[pl.BlockSpec(memory_space=pltpu.HBM)] * 4,
        out_specs=pl.BlockSpec(memory_space=pltpu.VMEM),
        scratch_shapes=[pltpu.SemaphoreType.DMA((4,))],
        compiler_params=pltpu.CompilerParams(vmem_limit_bytes=4 << 20),
        name="pack",
    )(*kept(*shards))


def frame_body(
    all_ref,
    gain_ref,
    qkv_ref,
    out_ref,
    result_ref,
    weight_ref,
    mix_ref,
    normed_ref,
    kv_ref,
    sems,
    *mixing,
):
    inner = kv_ref.shape[1] // 2
    band = lax.axis_index("band")
    waits = {}
    for order, part in enumerate((1, 2, 0)):
        columns = slice(part * inner, (part + 1) * inner)
        waits[part] = started(
            [pltpu.make_async_copy(qkv_ref.at[:, columns], weight_ref.at[:, columns], sems.at[order])]
        )
    mix = started([pltpu.make_async_copy(out_ref, mix_ref, sems.at[3])])
    project(all_ref, gain_ref, waits, weight_ref, normed_ref, kv_ref)
    mix()
    _, tokens, _ = all_ref.shape
    mixed(chunk_of(normed_ref, band, tokens), weight_ref, kv_ref, *mixing)
    update = jnp.dot(mixing[-1][...], mix_ref[...], preferred_element_type=jnp.float32)
    result_ref[...] = (all_ref[band].astype(jnp.float32) + update).astype(jnp.bfloat16)


def kept(*arrays):
    return [pltpu.with_memory_space_constraint(array, pltpu.HBM) for array in arrays]


def frame_layer(everything, gain, qkv, out):
    chunks, tokens, width = everything.shape
    inner = out.shape[0]
    count = chunks * tokens
    vmem = pl.BlockSpec(memory_space=pltpu.VMEM)
    hbm = pl.BlockSpec(memory_space=pltpu.HBM)
    return pl.pallas_call(
        frame_body,
        out_shape=jax.ShapeDtypeStruct((tokens, width), jnp.bfloat16),
        in_specs=[vmem, vmem, hbm, hbm],
        out_specs=vmem,
        scratch_shapes=[
            pltpu.VMEM((width, 3 * inner), jnp.bfloat16),
            pltpu.VMEM((inner, width), jnp.bfloat16),
            pltpu.VMEM((count, width), jnp.bfloat16),
            pltpu.VMEM((count, 2 * inner), jnp.bfloat16),
            pltpu.SemaphoreType.DMA((4,)),
        ]
        + mixing_scratch(tokens, count, inner),
        compiler_params=pltpu.CompilerParams(vmem_limit_bytes=20 << 20),
        cost_estimate=estimate(chunks, tokens, width, inner),
        name="frame",
    )(everything, gain, *kept(qkv, out))


def estimate(chunks, tokens, width, inner):
    count = chunks * tokens
    return pl.CostEstimate(
        flops=4 * count * width * inner + 4 * tokens * width * inner + 4 * tokens * count * inner,
        bytes_accessed=2 * (count * width + 4 * width * inner),
        transcendentals=tokens * count * inner // HEAD_DIM,
    )


def assembled(parts, weight_ref, sems, band, bands, core):
    qkv_ref, out_ref, near_ref, far_ref, other_near_ref, other_far_ref = parts
    inner = out_ref.shape[1]
    rows = far_ref.shape[0]

    def place(index, half, count):
        return pl.ds(pl.multiple_of((2 * lax.rem(index, bands) + half) * rows, rows), count)

    down, up = band + bands - 1, band + 1
    target = (
        place(band, 0, 2 * rows),
        place(down + 2 * core, 0, 2 * rows),
        place(band + 2, core, rows),
        place(up + 2 * core, 0, 2 * rows),
        place(band + 2, 1 - core, rows),
    )
    waits = {}
    for order, part in enumerate((1, 2, 0, 3)):
        columns = slice(part * inner, (part + 1) * inner)
        sources = (
            out_ref if part == 3 else qkv_ref.at[:, columns],
            near_ref.at[:, columns],
            far_ref.at[:, columns],
            other_near_ref.at[:, columns],
            other_far_ref.at[:, columns],
        )
        waits[part] = started(
            [
                pltpu.make_async_copy(source, weight_ref.at[goal, columns], sems.at[order, index])
                for index, (source, goal) in enumerate(zip(sources, target))
            ]
        )
    return waits


def rows_body(all_ref, gain1_ref, gain2_ref, *refs):
    shards, moved, refs = refs[:4], refs[4:8], refs[8:]
    parts1 = (*shards[:2], *(ref.at[0] for ref in moved))
    parts2 = (*shards[2:], *(ref.at[1] for ref in moved))
    result_ref, weight1_ref, weight2_ref, normed_ref, kv_ref, stream_ref, sems = refs[:7]
    mixing1, mixing2 = refs[7:12], refs[12:]
    chunks = all_ref.shape[0]
    inner = kv_ref.shape[1] // 2
    bands = lax.axis_size("band")
    band = lax.axis_index("band")
    core = lax.rem(lax.axis_index("batch"), 2)
    view = lax.axis_index("view")
    deep = lax.axis_size("view") // 2
    left = lax.rem(view, 2)
    own = jnp.where(view < deep, left, chunks - 1 - left)
    contract = (((1,), (1,)), ((), ()))
    waits1 = assembled(parts1, weight1_ref, sems.at[0], band, bands, core)
    waits2 = assembled(parts2, weight2_ref, sems.at[1], band, bands, core)
    project(all_ref, gain1_ref, waits1, weight1_ref, normed_ref, kv_ref)
    _, tokens, _ = all_ref.shape
    mixed(normed_ref[...], weight1_ref, kv_ref, *mixing1)
    waits1[3]()
    update = lax.dot_general(
        mixing1[-1][...], weight1_ref[:, 3 * inner :], contract, preferred_element_type=jnp.float32
    )
    for chunk in range(chunks):
        stream_ref[chunk] = (
            all_ref[chunk].astype(jnp.float32) + update[chunk * tokens : (chunk + 1) * tokens]
        ).astype(jnp.bfloat16)
    project(stream_ref, gain2_ref, waits2, weight2_ref, normed_ref, kv_ref)
    mixed(chunk_of(normed_ref, own, tokens), weight2_ref, kv_ref, *mixing2)
    waits2[3]()
    update = lax.dot_general(
        mixing2[-1][...], weight2_ref[:, 3 * inner :], contract, preferred_element_type=jnp.float32
    )
    result_ref[...] = (stream_ref[own].astype(jnp.float32) + update).astype(jnp.bfloat16)


def rows_layer(everything, gain1, gain2, weights):
    chunks, tokens, width = everything.shape
    inner = weights[1].shape[1]
    count = chunks * tokens
    vmem = pl.BlockSpec(memory_space=pltpu.VMEM)
    return pl.pallas_call(
        rows_body,
        out_shape=jax.ShapeDtypeStruct((tokens, width), jnp.bfloat16),
        in_specs=[vmem] * 3 + [pl.BlockSpec(memory_space=pltpu.HBM)] * 8,
        out_specs=vmem,
        scratch_shapes=[
            pltpu.VMEM((width, 4 * inner), jnp.bfloat16),
            pltpu.VMEM((width, 4 * inner), jnp.bfloat16),
            pltpu.VMEM((count, width), jnp.bfloat16),
            pltpu.VMEM((count, 2 * inner), jnp.bfloat16),
            pltpu.VMEM((chunks, tokens, width), jnp.bfloat16),
            pltpu.SemaphoreType.DMA((2, 4, 5)),
        ]
        + mixing_scratch(count, count, inner)
        + mixing_scratch(tokens, count, inner),
        compiler_params=pltpu.CompilerParams(vmem_limit_bytes=32 << 20),
        cost_estimate=estimate(chunks, tokens, width, inner),
        name="rows",
    )(everything, gain1, gain2, *kept(*weights))


def exchanged(stream, rows, groups):
    tokens, width = stream.shape
    return lax.all_to_all(
        stream.reshape(rows, tokens // rows, width),
        "view",
        split_axis=0,
        concat_axis=0,
        tiled=True,
        axis_index_groups=groups,
    ).reshape(tokens, width)


def layers(
    images,
    frame_gain,
    frame_qkv,
    frame_out,
    row1_gain,
    row1_qkv,
    row1_out,
    row2_gain,
    row2_qkv,
    row2_out,
):
    _, row_count, col_count, width = images.shape
    tokens = row_count * col_count
    views = lax.axis_size("view")
    bands = lax.axis_size("band")
    batches = lax.axis_size("batch")
    share = views // row_count
    near = 2
    deep = views // near
    side = share // near
    spread = [
        [y * deep + h * side + l for h in range(row_count)] for y in range(near) for l in range(side)
    ]
    ring = [
        [h * side + l for l in range(side)] + [deep + h * side + l for l in reversed(range(side))]
        for h in range(row_count)
    ]
    siblings = [(i, i ^ 1) for i in range(batches)]
    turn = [
        (b * batches + c, ((b + 1 - 2 * (c % 2)) % bands) * batches + c)
        for b in range(bands)
        for c in range(batches)
    ]

    shards = (row1_qkv, row1_out.T, row2_qkv, row2_out.T)
    core = lax.rem(lax.axis_index("batch"), 2)
    everything = lax.all_gather(images.reshape(tokens, width), "band", axis=0, tiled=False)
    everything, near = lax.optimization_barrier((everything, pack_layer(shards)))
    near = lax.ppermute(near, ("band", "batch"), turn)
    stream = frame_layer(everything, frame_gain, frame_qkv, frame_out)
    stream = exchanged(stream, row_count, spread)
    half = near.shape[1] // 2
    far = lax.dynamic_slice_in_dim(near, core * half, half, axis=1)
    far = lax.ppermute(far, ("band", "batch"), turn)
    other_near = lax.ppermute(near, "batch", siblings)
    gain1 = row1_gain.reshape(1, width)
    gain2 = row2_gain.reshape(1, width)
    other_far = lax.ppermute(far, "batch", siblings)
    everything = lax.all_gather(stream, "view", axis=0, tiled=False, axis_index_groups=ring)
    stream = rows_layer(
        everything, gain1, gain2, (*shards, near, far, other_near, other_far)
    )
    stream = exchanged(stream, row_count, spread)
    return stream.reshape(images.shape)


def solution(mesh):
    in_specs = (
        P(("batch", "view"), "band", None, None),
        P(),
        P(),
        P(),
        P(),
        P("band", None),
        P(None, "band"),
        P(),
        P("band", None),
        P(None, "band"),
    )
    out_specs = P(("batch", "view"), "band", None, None)
    return jax.shard_map(layers, mesh=mesh, in_specs=in_specs, out_specs=out_specs, check_vma=False)
```

```python
import math

import jax
import jax.numpy as jnp
from jax import lax
from jax.experimental import pallas as pl
from jax.experimental.pallas import tpu as pltpu
from jax.sharding import PartitionSpec as P


HEAD_DIM = 64
EPSILON = 1e-06
PAIR = 2 * HEAD_DIM
SCALE = HEAD_DIM ** (-0.5) * math.log2(math.e)
NORM_ROWS = 32
SOFTMAX_ROWS = 32


def project(all_ref, gain_ref, waits, weight_ref, normed_ref, kv_ref):
    chunks, tokens, width = all_ref.shape
    inner = kv_ref.shape[1] // 2
    gain = gain_ref[...].reshape(1, width)
    for chunk in range(chunks):
        for start in range(0, tokens, NORM_ROWS):
            values = all_ref[chunk, start : start + NORM_ROWS].astype(jnp.float32)
            factor = lax.rsqrt(jnp.mean(values * values, axis=-1, keepdims=True) + EPSILON)
            at = chunk * tokens + start
            normed_ref[at : at + NORM_ROWS, :] = (values * factor * gain).astype(jnp.bfloat16)
    for part in range(2):
        waits[1 + part]()
        kv_ref[:, part * inner : (part + 1) * inner] = jnp.dot(
            normed_ref[...],
            weight_ref[:, (1 + part) * inner : (2 + part) * inner],
            preferred_element_type=jnp.float32,
        ).astype(jnp.bfloat16)
    waits[0]()


def mixed(normed, weight_ref, kv_ref, query_ref, score_ref, rounded_ref, inverse_ref, attended_ref):
    count = normed.shape[0]
    inner = kv_ref.shape[1] // 2
    queries = (
        jnp.dot(normed, weight_ref[:, :inner], preferred_element_type=jnp.float32) * SCALE
    ).astype(jnp.bfloat16)
    first = lax.broadcasted_iota(jnp.int32, (count, PAIR), 1) < HEAD_DIM
    zeros = jnp.zeros((count, PAIR), jnp.bfloat16)
    for pair in range(inner // PAIR):
        query = queries[:, pair * PAIR : (pair + 1) * PAIR]
        query_ref[pair, :count] = jnp.where(first, query, zeros)
        query_ref[pair, count:] = jnp.where(first, zeros, query)
    for pair in range(inner // PAIR):
        slot = pair % 2
        columns = slice(pair * PAIR, (pair + 1) * PAIR)
        score_ref[slot] = lax.dot_general(
            query_ref[pair],
            kv_ref[:, columns],
            (((1,), (1,)), ((), ())),
            preferred_element_type=jnp.float32,
        )
        for start in range(0, 2 * count, SOFTMAX_ROWS):
            rows = slice(start, start + SOFTMAX_ROWS)
            scores = score_ref[slot, rows]
            weights = jnp.exp2(scores - jnp.max(scores, axis=-1, keepdims=True))
            total = jnp.sum(weights, axis=-1, keepdims=True)
            rounded_ref[slot, rows] = weights.astype(jnp.bfloat16)
            inverse_ref[slot, rows] = jnp.broadcast_to(1.0 / total, (SOFTMAX_ROWS, PAIR))
        result = inverse_ref[slot] * jnp.dot(
            rounded_ref[slot],
            kv_ref[:, inner + pair * PAIR : inner + (pair + 1) * PAIR],
            preferred_element_type=jnp.float32,
        )
        attended_ref[:, columns] = jnp.where(first, result[:count], result[count:]).astype(
            jnp.bfloat16
        )


def mixing_scratch(count, keys, inner):
    pairs = inner // PAIR
    return [
        pltpu.VMEM((pairs, 2 * count, PAIR), jnp.bfloat16),
        pltpu.VMEM((2, 2 * count, keys), jnp.float32),
        pltpu.VMEM((2, 2 * count, keys), jnp.bfloat16),
        pltpu.VMEM((2, 2 * count, PAIR), jnp.float32),
        pltpu.VMEM((count, inner), jnp.bfloat16),
    ]


def chunk_of(normed_ref, own, tokens):
    return normed_ref[pl.ds(pl.multiple_of(own * tokens, tokens), tokens), :]


def started(copies):
    for copy in copies:
        copy.start()

    def wait():
        for copy in copies:
            copy.wait()

    return wait


def pack_body(*refs):
    shards, near_ref, sems = refs[:4], refs[4], refs[5]
    columns = shards[0].shape[1]
    copies = []
    for layer in range(2):
        qkv, out = shards[2 * layer : 2 * layer + 2]
        copies.append(
            pltpu.make_async_copy(qkv, near_ref.at[layer, :, :columns], sems.at[2 * layer])
        )
        copies.append(
            pltpu.make_async_copy(out, near_ref.at[layer, :, columns:], sems.at[2 * layer + 1])
        )
    started(copies)()


def pack_layer(shards):
    qkv, out = shards[:2]
    return pl.pallas_call(
        pack_body,
        out_shape=jax.ShapeDtypeStruct((2, qkv.shape[0], qkv.shape[1] + out.shape[1]), jnp.bfloat16),
        in_specs=[pl.BlockSpec(memory_space=pltpu.HBM)] * 4,
        out_specs=pl.BlockSpec(memory_space=pltpu.VMEM),
        scratch_shapes=[pltpu.SemaphoreType.DMA((4,))],
        compiler_params=pltpu.CompilerParams(vmem_limit_bytes=4 << 20),
        name="pack",
    )(*kept(*shards))


def frame_body(
    all_ref,
    gain_ref,
    qkv_ref,
    out_ref,
    result_ref,
    weight_ref,
    mix_ref,
    normed_ref,
    kv_ref,
    sems,
    *mixing,
):
    inner = kv_ref.shape[1] // 2
    band = lax.axis_index("band")
    waits = {}
    for order, part in enumerate((1, 2, 0)):
        columns = slice(part * inner, (part + 1) * inner)
        waits[part] = started(
            [pltpu.make_async_copy(qkv_ref.at[:, columns], weight_ref.at[:, columns], sems.at[order])]
        )
    mix = started([pltpu.make_async_copy(out_ref, mix_ref, sems.at[3])])
    project(all_ref, gain_ref, waits, weight_ref, normed_ref, kv_ref)
    mix()
    _, tokens, _ = all_ref.shape
    mixed(chunk_of(normed_ref, band, tokens), weight_ref, kv_ref, *mixing)
    update = jnp.dot(mixing[-1][...], mix_ref[...], preferred_element_type=jnp.float32)
    result_ref[...] = (all_ref[band].astype(jnp.float32) + update).astype(jnp.bfloat16)


def kept(*arrays):
    return [pltpu.with_memory_space_constraint(array, pltpu.HBM) for array in arrays]


def frame_layer(everything, gain, qkv, out):
    chunks, tokens, width = everything.shape
    inner = out.shape[0]
    count = chunks * tokens
    vmem = pl.BlockSpec(memory_space=pltpu.VMEM)
    hbm = pl.BlockSpec(memory_space=pltpu.HBM)
    return pl.pallas_call(
        frame_body,
        out_shape=jax.ShapeDtypeStruct((tokens, width), jnp.bfloat16),
        in_specs=[vmem, vmem, hbm, hbm],
        out_specs=vmem,
        scratch_shapes=[
            pltpu.VMEM((width, 3 * inner), jnp.bfloat16),
            pltpu.VMEM((inner, width), jnp.bfloat16),
            pltpu.VMEM((count, width), jnp.bfloat16),
            pltpu.VMEM((count, 2 * inner), jnp.bfloat16),
            pltpu.SemaphoreType.DMA((4,)),
        ]
        + mixing_scratch(tokens, count, inner),
        compiler_params=pltpu.CompilerParams(vmem_limit_bytes=20 << 20),
        cost_estimate=estimate(chunks, tokens, width, inner),
        name="frame",
    )(everything, gain, *kept(qkv, out))


def estimate(chunks, tokens, width, inner):
    count = chunks * tokens
    return pl.CostEstimate(
        flops=4 * count * width * inner + 4 * tokens * width * inner + 4 * tokens * count * inner,
        bytes_accessed=2 * (count * width + 4 * width * inner),
        transcendentals=tokens * count * inner // HEAD_DIM,
    )


def assembled(parts, weight_ref, sems, band, bands, core):
    qkv_ref, out_ref, near_ref, far_ref, other_near_ref, other_far_ref = parts
    inner = out_ref.shape[1]
    rows = far_ref.shape[0]

    def place(index, half, count):
        return pl.ds(pl.multiple_of((2 * lax.rem(index, bands) + half) * rows, rows), count)

    down, up = band + bands - 1, band + 1
    target = (
        place(band, 0, 2 * rows),
        place(down + 2 * core, 0, 2 * rows),
        place(band + 2, core, rows),
        place(up + 2 * core, 0, 2 * rows),
        place(band + 2, 1 - core, rows),
    )
    waits = {}
    for order, part in enumerate((1, 2, 0, 3)):
        columns = slice(part * inner, (part + 1) * inner)
        sources = (
            out_ref if part == 3 else qkv_ref.at[:, columns],
            near_ref.at[:, columns],
            far_ref.at[:, columns],
            other_near_ref.at[:, columns],
            other_far_ref.at[:, columns],
        )
        waits[part] = started(
            [
                pltpu.make_async_copy(source, weight_ref.at[goal, columns], sems.at[order, index])
                for index, (source, goal) in enumerate(zip(sources, target))
            ]
        )
    return waits


def rows_body(all_ref, gain1_ref, gain2_ref, *refs):
    shards, moved, refs = refs[:4], refs[4:8], refs[8:]
    parts1 = (*shards[:2], *(ref.at[0] for ref in moved))
    parts2 = (*shards[2:], *(ref.at[1] for ref in moved))
    result_ref, weight1_ref, weight2_ref, normed_ref, kv_ref, stream_ref, sems = refs[:7]
    mixing1, mixing2 = refs[7:12], refs[12:]
    chunks = all_ref.shape[0]
    inner = kv_ref.shape[1] // 2
    bands = lax.axis_size("band")
    band = lax.axis_index("band")
    core = lax.rem(lax.axis_index("batch"), 2)
    view = lax.axis_index("view")
    deep = lax.axis_size("view") // 2
    left = lax.rem(view, 2)
    own = jnp.where(view < deep, left, chunks - 1 - left)
    contract = (((1,), (1,)), ((), ()))
    waits1 = assembled(parts1, weight1_ref, sems.at[0], band, bands, core)
    waits2 = assembled(parts2, weight2_ref, sems.at[1], band, bands, core)
    project(all_ref, gain1_ref, waits1, weight1_ref, normed_ref, kv_ref)
    _, tokens, _ = all_ref.shape
    mixed(normed_ref[...], weight1_ref, kv_ref, *mixing1)
    waits1[3]()
    update = lax.dot_general(
        mixing1[-1][...], weight1_ref[:, 3 * inner :], contract, preferred_element_type=jnp.float32
    )
    for chunk in range(chunks):
        stream_ref[chunk] = (
            all_ref[chunk].astype(jnp.float32) + update[chunk * tokens : (chunk + 1) * tokens]
        ).astype(jnp.bfloat16)
    project(stream_ref, gain2_ref, waits2, weight2_ref, normed_ref, kv_ref)
    mixed(chunk_of(normed_ref, own, tokens), weight2_ref, kv_ref, *mixing2)
    waits2[3]()
    update = lax.dot_general(
        mixing2[-1][...], weight2_ref[:, 3 * inner :], contract, preferred_element_type=jnp.float32
    )
    result_ref[...] = (stream_ref[own].astype(jnp.float32) + update).astype(jnp.bfloat16)


def rows_layer(everything, gain1, gain2, weights):
    chunks, tokens, width = everything.shape
    inner = weights[1].shape[1]
    count = chunks * tokens
    vmem = pl.BlockSpec(memory_space=pltpu.VMEM)
    return pl.pallas_call(
        rows_body,
        out_shape=jax.ShapeDtypeStruct((tokens, width), jnp.bfloat16),
        in_specs=[vmem] * 3 + [pl.BlockSpec(memory_space=pltpu.HBM)] * 8,
        out_specs=vmem,
        scratch_shapes=[
            pltpu.VMEM((width, 4 * inner), jnp.bfloat16),
            pltpu.VMEM((width, 4 * inner), jnp.bfloat16),
            pltpu.VMEM((count, width), jnp.bfloat16),
            pltpu.VMEM((count, 2 * inner), jnp.bfloat16),
            pltpu.VMEM((chunks, tokens, width), jnp.bfloat16),
            pltpu.SemaphoreType.DMA((2, 4, 5)),
        ]
        + mixing_scratch(count, count, inner)
        + mixing_scratch(tokens, count, inner),
        compiler_params=pltpu.CompilerParams(vmem_limit_bytes=32 << 20),
        cost_estimate=estimate(chunks, tokens, width, inner),
        name="rows",
    )(everything, gain1, gain2, *kept(*weights))


def exchanged(stream, rows, groups):
    tokens, width = stream.shape
    return lax.all_to_all(
        stream.reshape(rows, tokens // rows, width),
        "view",
        split_axis=0,
        concat_axis=0,
        tiled=True,
        axis_index_groups=groups,
    ).reshape(tokens, width)


def layers(
    images,
    frame_gain,
    frame_qkv,
    frame_out,
    row1_gain,
    row1_qkv,
    row1_out,
    row2_gain,
    row2_qkv,
    row2_out,
):
    _, row_count, col_count, width = images.shape
    tokens = row_count * col_count
    views = lax.axis_size("view")
    bands = lax.axis_size("band")
    batches = lax.axis_size("batch")
    share = views // row_count
    near = 2
    deep = views // near
    side = share // near
    spread = [
        [y * deep + h * side + l for h in range(row_count)] for y in range(near) for l in range(side)
    ]
    ring = [
        [h * side + l for l in range(side)] + [deep + h * side + l for l in reversed(range(side))]
        for h in range(row_count)
    ]
    siblings = [(i, i ^ 1) for i in range(batches)]
    turn = [
        (b * batches + c, ((b + 1 - 2 * (c % 2)) % bands) * batches + c)
        for b in range(bands)
        for c in range(batches)
    ]

    shards = (row1_qkv, row1_out.T, row2_qkv, row2_out.T)
    core = lax.rem(lax.axis_index("batch"), 2)
    everything = lax.all_gather(images.reshape(tokens, width), "band", axis=0, tiled=False)
    everything, near = lax.optimization_barrier((everything, pack_layer(shards)))
    near = lax.ppermute(near, ("band", "batch"), turn)
    stream = frame_layer(everything, frame_gain, frame_qkv, frame_out)
    stream = exchanged(stream, row_count, spread)
    half = near.shape[1] // 2
    far = lax.dynamic_slice_in_dim(near, core * half, half, axis=1)
    far = lax.ppermute(far, ("band", "batch"), turn)
    other_near = lax.ppermute(near, "batch", siblings)
    gain1 = row1_gain.reshape(1, width)
    gain2 = row2_gain.reshape(1, width)
    other_far = lax.ppermute(far, "batch", siblings)
    everything = lax.all_to_all(
        jnp.broadcast_to(stream[None], (share, tokens, width)),
        "view",
        split_axis=0,
        concat_axis=0,
        tiled=True,
        axis_index_groups=ring,
    )
    stream = rows_layer(
        everything, gain1, gain2, (*shards, near, far, other_near, other_far)
    )
    stream = exchanged(stream, row_count, spread)
    return stream.reshape(images.shape)


def solution(mesh):
    in_specs = (
        P(("batch", "view"), "band", None, None),
        P(),
        P(),
        P(),
        P(),
        P("band", None),
        P(None, "band"),
        P(),
        P("band", None),
        P(None, "band"),
    )
    out_specs = P(("batch", "view"), "band", None, None)
    return jax.shard_map(layers, mesh=mesh, in_specs=in_specs, out_specs=out_specs, check_vma=False)
```

```python
import math

import jax
import jax.numpy as jnp
from jax import lax
from jax.experimental import pallas as pl
from jax.experimental.pallas import tpu as pltpu
from jax.sharding import PartitionSpec as P


HEAD_DIM = 64
EPSILON = 1e-06
PAIR = 2 * HEAD_DIM
SCALE = HEAD_DIM ** (-0.5) * math.log2(math.e)
NORM_ROWS = 32
SOFTMAX_ROWS = 32


def project(all_ref, gain_ref, waits, weight_ref, normed_ref, kv_ref):
    chunks, tokens, width = all_ref.shape
    inner = kv_ref.shape[1] // 2
    gain = gain_ref[...].reshape(1, width)
    for chunk in range(chunks):
        for start in range(0, tokens, NORM_ROWS):
            values = all_ref[chunk, start : start + NORM_ROWS].astype(jnp.float32)
            factor = lax.rsqrt(jnp.mean(values * values, axis=-1, keepdims=True) + EPSILON)
            at = chunk * tokens + start
            normed_ref[at : at + NORM_ROWS, :] = (values * factor * gain).astype(jnp.bfloat16)
    for part in range(2):
        if waits:
            waits[1 + part]()
        kv_ref[:, part * inner : (part + 1) * inner] = jnp.dot(
            normed_ref[...],
            weight_ref[:, (1 + part) * inner : (2 + part) * inner],
            preferred_element_type=jnp.float32,
        ).astype(jnp.bfloat16)
    if waits:
        waits[0]()


def mixed(fence, read_normed, weight_ref, kv_ref, query_ref, score_ref, rounded_ref, inverse_ref, attended_ref):
    count = attended_ref.shape[0]
    inner = kv_ref.shape[1] // 2
    pairs = inner // PAIR

    @pl.when(fence)
    def _():
        first = lax.broadcasted_iota(jnp.int32, (count, PAIR), 1) < HEAD_DIM
        zeros = jnp.zeros((count, PAIR), jnp.bfloat16)
        queries = (
            jnp.dot(read_normed(), weight_ref[:, :inner], preferred_element_type=jnp.float32) * SCALE
        ).astype(jnp.bfloat16)
        for pair in range(pairs):
            query = queries[:, pair * PAIR : (pair + 1) * PAIR]
            query_ref[pair, :count] = jnp.where(first, query, zeros)
            query_ref[pair, count:] = jnp.where(first, zeros, query)

    def score(pair):
        score_ref[pair % 2] = lax.dot_general(
            query_ref[pair],
            kv_ref[:, pair * PAIR : (pair + 1) * PAIR],
            (((1,), (1,)), ((), ())),
            preferred_element_type=jnp.float32,
        )

    def weigh(pair):
        slot = pair % 2
        for start in range(0, 2 * count, SOFTMAX_ROWS):
            rows = slice(start, start + SOFTMAX_ROWS)
            scores = score_ref[slot, rows]
            weights = jnp.exp2(scores - jnp.max(scores, axis=-1, keepdims=True))
            total = jnp.sum(weights, axis=-1, keepdims=True)
            rounded_ref[slot, rows] = weights.astype(jnp.bfloat16)
            inverse_ref[slot, rows] = jnp.broadcast_to(1.0 / total, (SOFTMAX_ROWS, PAIR))

    def mix(pair):
        slot = pair % 2
        first = lax.broadcasted_iota(jnp.int32, (count, PAIR), 1) < HEAD_DIM
        result = inverse_ref[slot] * jnp.dot(
            rounded_ref[slot],
            kv_ref[:, inner + pair * PAIR : inner + (pair + 1) * PAIR],
            preferred_element_type=jnp.float32,
        )
        attended_ref[:, pair * PAIR : (pair + 1) * PAIR] = jnp.where(
            first, result[:count], result[count:]
        ).astype(jnp.bfloat16)

    for stage in range(pairs + 2):

        @pl.when(fence)
        def _(stage=stage):
            if stage < pairs:
                score(stage)
            if 0 <= stage - 1 < pairs:
                weigh(stage - 1)
            if 0 <= stage - 2:
                mix(stage - 2)


def mixing_scratch(count, keys, inner):
    pairs = inner // PAIR
    return [
        pltpu.VMEM((pairs, 2 * count, PAIR), jnp.bfloat16),
        pltpu.VMEM((2, 2 * count, keys), jnp.float32),
        pltpu.VMEM((2, 2 * count, keys), jnp.bfloat16),
        pltpu.VMEM((2, 2 * count, PAIR), jnp.float32),
        pltpu.VMEM((count, inner), jnp.bfloat16),
    ]


def chunk_of(normed_ref, own, tokens):
    return normed_ref[pl.ds(pl.multiple_of(own * tokens, tokens), tokens), :]


def started(copies):
    for copy in copies:
        copy.start()

    def wait():
        for copy in copies:
            copy.wait()

    return wait


def pack_body(*refs):
    shards, near_ref, sems = refs[:4], refs[4], refs[5]
    columns = shards[0].shape[1]
    copies = []
    for layer in range(2):
        qkv, out = shards[2 * layer : 2 * layer + 2]
        copies.append(
            pltpu.make_async_copy(qkv, near_ref.at[layer, :, :columns], sems.at[2 * layer])
        )
        copies.append(
            pltpu.make_async_copy(out, near_ref.at[layer, :, columns:], sems.at[2 * layer + 1])
        )
    started(copies)()


def pack_layer(shards):
    qkv, out = shards[:2]
    return pl.pallas_call(
        pack_body,
        out_shape=jax.ShapeDtypeStruct((2, qkv.shape[0], qkv.shape[1] + out.shape[1]), jnp.bfloat16),
        in_specs=[pl.BlockSpec(memory_space=pltpu.HBM)] * 4,
        out_specs=pl.BlockSpec(memory_space=pltpu.VMEM),
        scratch_shapes=[pltpu.SemaphoreType.DMA((4,))],
        compiler_params=pltpu.CompilerParams(vmem_limit_bytes=4 << 20),
        name="pack",
    )(*kept(*shards))


def frame_body(
    all_ref,
    gain_ref,
    qkv_ref,
    out_ref,
    result_ref,
    weight_ref,
    mix_ref,
    normed_ref,
    kv_ref,
    sems,
    *mixing,
):
    inner = kv_ref.shape[1] // 2
    band = lax.axis_index("band")
    waits = {}
    for order, part in enumerate((1, 2, 0)):
        columns = slice(part * inner, (part + 1) * inner)
        waits[part] = started(
            [pltpu.make_async_copy(qkv_ref.at[:, columns], weight_ref.at[:, columns], sems.at[order])]
        )
    mix = started([pltpu.make_async_copy(out_ref, mix_ref, sems.at[3])])
    project(all_ref, gain_ref, waits, weight_ref, normed_ref, kv_ref)
    mix()
    _, tokens, _ = all_ref.shape
    mixed(band >= 0, lambda: chunk_of(normed_ref, band, tokens), weight_ref, kv_ref, *mixing)
    update = jnp.dot(mixing[-1][...], mix_ref[...], preferred_element_type=jnp.float32)
    result_ref[...] = (all_ref[band].astype(jnp.float32) + update).astype(jnp.bfloat16)


def kept(*arrays):
    return [pltpu.with_memory_space_constraint(array, pltpu.HBM) for array in arrays]


def frame_layer(everything, gain, qkv, out):
    chunks, tokens, width = everything.shape
    inner = out.shape[0]
    count = chunks * tokens
    vmem = pl.BlockSpec(memory_space=pltpu.VMEM)
    hbm = pl.BlockSpec(memory_space=pltpu.HBM)
    return pl.pallas_call(
        frame_body,
        out_shape=jax.ShapeDtypeStruct((tokens, width), jnp.bfloat16),
        in_specs=[vmem, vmem, hbm, hbm],
        out_specs=vmem,
        scratch_shapes=[
            pltpu.VMEM((width, 3 * inner), jnp.bfloat16),
            pltpu.VMEM((inner, width), jnp.bfloat16),
            pltpu.VMEM((count, width), jnp.bfloat16),
            pltpu.VMEM((count, 2 * inner), jnp.bfloat16),
            pltpu.SemaphoreType.DMA((4,)),
        ]
        + mixing_scratch(tokens, count, inner),
        compiler_params=pltpu.CompilerParams(vmem_limit_bytes=20 << 20),
        cost_estimate=estimate(chunks, tokens, width, inner),
        name="frame",
    )(everything, gain, *kept(qkv, out))


def estimate(chunks, tokens, width, inner):
    count = chunks * tokens
    return pl.CostEstimate(
        flops=4 * count * width * inner + 4 * tokens * width * inner + 4 * tokens * count * inner,
        bytes_accessed=2 * (count * width + 4 * width * inner),
        transcendentals=tokens * count * inner // HEAD_DIM,
    )


def assembled(parts, weight_ref, sems, band, bands, core):
    inner = parts[1].shape[1]
    rows = parts[1].shape[0]
    target = [
        pl.ds(pl.multiple_of(lax.rem(band + step, bands) * rows, rows), rows)
        for step in (0, bands - 1 + 2 * core, 2, 1 + 2 * core)
    ]
    waits = {}
    for order, part in enumerate((1, 2, 0, 3)):
        columns = slice(part * inner, (part + 1) * inner)
        sources = (parts[1] if part == 3 else parts[0].at[:, columns],)
        sources += tuple(ref.at[:, columns] for ref in parts[2:])
        waits[part] = started(
            [
                pltpu.make_async_copy(source, weight_ref.at[goal, columns], sems.at[order, index])
                for index, (source, goal) in enumerate(zip(sources, target))
            ]
        )
    return waits


def rows_body(all_ref, gain1_ref, gain2_ref, *refs):
    shards, moved, refs = refs[:4], refs[4:7], refs[7:]
    parts1 = (*shards[:2], *(ref.at[0] for ref in moved))
    parts2 = (*shards[2:], *(ref.at[1] for ref in moved))
    result_ref, weight1_ref, weight2_ref, normed_ref, kv_ref, stream_ref, sems = refs[:7]
    mixing1, mixing2 = refs[7:12], refs[12:]
    chunks = all_ref.shape[0]
    inner = kv_ref.shape[1] // 2
    bands = lax.axis_size("band")
    band = lax.axis_index("band")
    core = lax.rem(lax.axis_index("batch"), 2)
    view = lax.axis_index("view")
    deep = lax.axis_size("view") // 2
    left = lax.rem(view, 2)
    own = jnp.where(view < deep, left, chunks - 1 - left)
    contract = (((1,), (1,)), ((), ()))
    waits1 = assembled(parts1, weight1_ref, sems.at[0], band, bands, core)
    waits2 = assembled(parts2, weight2_ref, sems.at[1], band, bands, core)
    project(all_ref, gain1_ref, waits1, weight1_ref, normed_ref, kv_ref)
    _, tokens, _ = all_ref.shape
    mixed(band >= 0, lambda: normed_ref[...], weight1_ref, kv_ref, *mixing1)
    waits1[3]()
    update = lax.dot_general(
        mixing1[-1][...], weight1_ref[:, 3 * inner :], contract, preferred_element_type=jnp.float32
    )
    for chunk in range(chunks):
        stream_ref[chunk] = (
            all_ref[chunk].astype(jnp.float32) + update[chunk * tokens : (chunk + 1) * tokens]
        ).astype(jnp.bfloat16)
    for part in range(4):
        waits2[part]()
    project(stream_ref, gain2_ref, None, weight2_ref, normed_ref, kv_ref)
    mixed(band >= 0, lambda: chunk_of(normed_ref, own, tokens), weight2_ref, kv_ref, *mixing2)
    update = lax.dot_general(
        mixing2[-1][...], weight2_ref[:, 3 * inner :], contract, preferred_element_type=jnp.float32
    )
    result_ref[...] = (stream_ref[own].astype(jnp.float32) + update).astype(jnp.bfloat16)


def rows_layer(everything, gain1, gain2, weights):
    chunks, tokens, width = everything.shape
    inner = weights[1].shape[1]
    count = chunks * tokens
    vmem = pl.BlockSpec(memory_space=pltpu.VMEM)
    return pl.pallas_call(
        rows_body,
        out_shape=jax.ShapeDtypeStruct((tokens, width), jnp.bfloat16),
        in_specs=[vmem] * 3 + [pl.BlockSpec(memory_space=pltpu.HBM)] * 7,
        out_specs=vmem,
        scratch_shapes=[
            pltpu.VMEM((width, 4 * inner), jnp.bfloat16),
            pltpu.VMEM((width, 4 * inner), jnp.bfloat16),
            pltpu.VMEM((count, width), jnp.bfloat16),
            pltpu.VMEM((count, 2 * inner), jnp.bfloat16),
            pltpu.VMEM((chunks, tokens, width), jnp.bfloat16),
            pltpu.SemaphoreType.DMA((2, 4, 4)),
        ]
        + mixing_scratch(count, count, inner)
        + mixing_scratch(tokens, count, inner),
        compiler_params=pltpu.CompilerParams(vmem_limit_bytes=32 << 20),
        cost_estimate=estimate(chunks, tokens, width, inner),
        name="rows",
    )(everything, gain1, gain2, *kept(*weights))


def exchanged(stream, rows, groups):
    tokens, width = stream.shape
    return lax.all_to_all(
        stream.reshape(rows, tokens // rows, width),
        "view",
        split_axis=0,
        concat_axis=0,
        tiled=True,
        axis_index_groups=groups,
    ).reshape(tokens, width)


def layers(
    images,
    frame_gain,
    frame_qkv,
    frame_out,
    row1_gain,
    row1_qkv,
    row1_out,
    row2_gain,
    row2_qkv,
    row2_out,
):
    _, row_count, col_count, width = images.shape
    tokens = row_count * col_count
    views = lax.axis_size("view")
    bands = lax.axis_size("band")
    batches = lax.axis_size("batch")
    share = views // row_count
    near = 2
    deep = views // near
    side = share // near
    spread = [
        [y * deep + h * side + l for h in range(row_count)] for y in range(near) for l in range(side)
    ]
    ring = [
        [h * side + l for l in range(side)] + [deep + h * side + l for l in reversed(range(side))]
        for h in range(row_count)
    ]
    siblings = [(i, i ^ 1) for i in range(batches)]
    turn = [
        (b * batches + c, ((b + 1 - 2 * (c % 2)) % bands) * batches + c)
        for b in range(bands)
        for c in range(batches)
    ]

    shards = (row1_qkv, row1_out.T, row2_qkv, row2_out.T)
    everything = lax.all_gather(images.reshape(tokens, width), "band", axis=0, tiled=False)
    everything, near = lax.optimization_barrier((everything, pack_layer(shards)))
    near = lax.ppermute(near, ("band", "batch"), turn)
    stream = frame_layer(everything, frame_gain, frame_qkv, frame_out)
    stream = exchanged(stream, row_count, spread)
    far = lax.ppermute(near, ("band", "batch"), turn)
    other = lax.ppermute(near, "batch", siblings)
    gain1 = row1_gain.reshape(1, width)
    gain2 = row2_gain.reshape(1, width)
    everything = lax.all_gather(stream, "view", axis=0, tiled=False, axis_index_groups=ring)
    stream = rows_layer(
        everything, gain1, gain2, (*shards, near, far, other)
    )
    stream = exchanged(stream, row_count, spread)
    return stream.reshape(images.shape)


def solution(mesh):
    in_specs = (
        P(("batch", "view"), "band", None, None),
        P(),
        P(),
        P(),
        P(),
        P("band", None),
        P(None, "band"),
        P(),
        P("band", None),
        P(None, "band"),
    )
    out_specs = P(("batch", "view"), "band", None, None)
    return jax.shard_map(layers, mesh=mesh, in_specs=in_specs, out_specs=out_specs, check_vma=False)
```

```python
import math

import jax
import jax.numpy as jnp
from jax import lax
from jax.experimental import pallas as pl
from jax.experimental.pallas import tpu as pltpu
from jax.sharding import PartitionSpec as P


HEAD_DIM = 64
EPSILON = 1e-06
PAIR = 2 * HEAD_DIM
SCALE = HEAD_DIM ** (-0.5) * math.log2(math.e)
NORM_ROWS = 32
SOFTMAX_ROWS = 32


def project(all_ref, gain_ref, waits, weight_ref, normed_ref, kv_ref):
    chunks, tokens, width = all_ref.shape
    inner = kv_ref.shape[1] // 2
    gain = gain_ref[...].reshape(1, width)
    for chunk in range(chunks):
        for start in range(0, tokens, NORM_ROWS):
            values = all_ref[chunk, start : start + NORM_ROWS].astype(jnp.float32)
            factor = lax.rsqrt(jnp.mean(values * values, axis=-1, keepdims=True) + EPSILON)
            at = chunk * tokens + start
            normed_ref[at : at + NORM_ROWS, :] = (values * factor * gain).astype(jnp.bfloat16)
    for part in range(2):
        if waits:
            waits[1 + part]()
        kv_ref[:, part * inner : (part + 1) * inner] = jnp.dot(
            normed_ref[...],
            weight_ref[:, (1 + part) * inner : (2 + part) * inner],
            preferred_element_type=jnp.float32,
        ).astype(jnp.bfloat16)
    if waits:
        waits[0]()


def mixed(fence, read_normed, weight_ref, kv_ref, query_ref, score_ref, rounded_ref, inverse_ref, attended_ref):
    count = attended_ref.shape[0]
    inner = kv_ref.shape[1] // 2
    pairs = inner // PAIR

    @pl.when(fence)
    def _():
        first = lax.broadcasted_iota(jnp.int32, (count, PAIR), 1) < HEAD_DIM
        zeros = jnp.zeros((count, PAIR), jnp.bfloat16)
        queries = (
            jnp.dot(read_normed(), weight_ref[:, :inner], preferred_element_type=jnp.float32) * SCALE
        ).astype(jnp.bfloat16)
        for pair in range(pairs):
            query = queries[:, pair * PAIR : (pair + 1) * PAIR]
            query_ref[pair, :count] = jnp.where(first, query, zeros)
            query_ref[pair, count:] = jnp.where(first, zeros, query)

    def score(pair):
        score_ref[pair % 2] = lax.dot_general(
            query_ref[pair],
            kv_ref[:, pair * PAIR : (pair + 1) * PAIR],
            (((1,), (1,)), ((), ())),
            preferred_element_type=jnp.float32,
        )

    def weigh(pair):
        slot = pair % 2
        for start in range(0, 2 * count, SOFTMAX_ROWS):
            rows = slice(start, start + SOFTMAX_ROWS)
            scores = score_ref[slot, rows]
            weights = jnp.exp2(scores - jnp.max(scores, axis=-1, keepdims=True))
            total = jnp.sum(weights, axis=-1, keepdims=True)
            rounded_ref[slot, rows] = weights.astype(jnp.bfloat16)
            inverse_ref[slot, rows] = jnp.broadcast_to(1.0 / total, (SOFTMAX_ROWS, PAIR))

    def mix(pair):
        slot = pair % 2
        first = lax.broadcasted_iota(jnp.int32, (count, PAIR), 1) < HEAD_DIM
        result = inverse_ref[slot] * jnp.dot(
            rounded_ref[slot],
            kv_ref[:, inner + pair * PAIR : inner + (pair + 1) * PAIR],
            preferred_element_type=jnp.float32,
        )
        attended_ref[:, pair * PAIR : (pair + 1) * PAIR] = jnp.where(
            first, result[:count], result[count:]
        ).astype(jnp.bfloat16)

    for stage in range(pairs + 2):

        @pl.when(fence)
        def _(stage=stage):
            if stage < pairs:
                score(stage)
            if 0 <= stage - 1 < pairs:
                weigh(stage - 1)
            if 0 <= stage - 2:
                mix(stage - 2)


def mixing_scratch(count, keys, inner):
    pairs = inner // PAIR
    return [
        pltpu.VMEM((pairs, 2 * count, PAIR), jnp.bfloat16),
        pltpu.VMEM((2, 2 * count, keys), jnp.float32),
        pltpu.VMEM((2, 2 * count, keys), jnp.bfloat16),
        pltpu.VMEM((2, 2 * count, PAIR), jnp.float32),
        pltpu.VMEM((count, inner), jnp.bfloat16),
    ]


def chunk_of(normed_ref, own, tokens):
    return normed_ref[pl.ds(pl.multiple_of(own * tokens, tokens), tokens), :]


def started(copies):
    for copy in copies:
        copy.start()

    def wait():
        for copy in copies:
            copy.wait()

    return wait


def pack_body(*refs):
    shards, nears, sems = refs[:4], refs[4:6], refs[6]
    columns = shards[0].shape[1]
    copies = []
    for layer in range(2):
        qkv, out = shards[2 * layer : 2 * layer + 2]
        copies.append(
            pltpu.make_async_copy(qkv, nears[layer].at[:, :columns], sems.at[2 * layer])
        )
        copies.append(
            pltpu.make_async_copy(out, nears[layer].at[:, columns:], sems.at[2 * layer + 1])
        )
    started(copies)()


def pack_layer(shards):
    qkv, out = shards[:2]
    return pl.pallas_call(
        pack_body,
        out_shape=(
            jax.ShapeDtypeStruct((qkv.shape[0], qkv.shape[1] + out.shape[1]), jnp.bfloat16),
        )
        * 2,
        in_specs=[pl.BlockSpec(memory_space=pltpu.HBM)] * 4,
        out_specs=(pl.BlockSpec(memory_space=pltpu.VMEM),) * 2,
        scratch_shapes=[pltpu.SemaphoreType.DMA((4,))],
        compiler_params=pltpu.CompilerParams(vmem_limit_bytes=4 << 20),
        name="pack",
    )(*kept(*shards))


def frame_body(
    all_ref,
    gain_ref,
    weight_ref,
    out_ref,
    result_ref,
    mix_ref,
    normed_ref,
    kv_ref,
    sem,
    *mixing,
):
    band = lax.axis_index("band")
    mix = started([pltpu.make_async_copy(out_ref, mix_ref, sem)])
    project(all_ref, gain_ref, None, weight_ref, normed_ref, kv_ref)
    _, tokens, _ = all_ref.shape
    mixed(band >= 0, lambda: chunk_of(normed_ref, band, tokens), weight_ref, kv_ref, *mixing)
    mix()
    update = jnp.dot(mixing[-1][...], mix_ref[...], preferred_element_type=jnp.float32)
    result_ref[...] = (all_ref[band].astype(jnp.float32) + update).astype(jnp.bfloat16)


def kept(*arrays):
    return [pltpu.with_memory_space_constraint(array, pltpu.HBM) for array in arrays]


def frame_layer(everything, gain, qkv, out):
    chunks, tokens, width = everything.shape
    inner = out.shape[0]
    count = chunks * tokens
    vmem = pl.BlockSpec(memory_space=pltpu.VMEM)
    return pl.pallas_call(
        frame_body,
        out_shape=jax.ShapeDtypeStruct((tokens, width), jnp.bfloat16),
        in_specs=[vmem] * 3 + [pl.BlockSpec(memory_space=pltpu.HBM)],
        out_specs=vmem,
        scratch_shapes=[
            pltpu.VMEM((inner, width), jnp.bfloat16),
            pltpu.VMEM((count, width), jnp.bfloat16),
            pltpu.VMEM((count, 2 * inner), jnp.bfloat16),
            pltpu.SemaphoreType.DMA,
        ]
        + mixing_scratch(tokens, count, inner),
        compiler_params=pltpu.CompilerParams(vmem_limit_bytes=20 << 20),
        cost_estimate=estimate(chunks, tokens, width, inner),
        name="frame",
    )(everything, gain, qkv, *kept(out))


def estimate(chunks, tokens, width, inner):
    count = chunks * tokens
    return pl.CostEstimate(
        flops=4 * count * width * inner + 4 * tokens * width * inner + 4 * tokens * count * inner,
        bytes_accessed=2 * (count * width + 4 * width * inner),
        transcendentals=tokens * count * inner // HEAD_DIM,
    )


def assembled(parts, weight_ref, sems, band, bands, core):
    inner = parts[1].shape[1]
    rows = parts[1].shape[0]
    target = [
        pl.ds(pl.multiple_of(lax.rem(band + step, bands) * rows, rows), rows)
        for step in (0, bands - 1 + 2 * core, 2, 1 + 2 * core)
    ]
    waits = {}
    for order, part in enumerate((1, 2, 0, 3)):
        columns = slice(part * inner, (part + 1) * inner)
        sources = (parts[1] if part == 3 else parts[0].at[:, columns],)
        sources += tuple(ref.at[:, columns] for ref in parts[2:])
        waits[part] = started(
            [
                pltpu.make_async_copy(source, weight_ref.at[goal, columns], sems.at[order, index])
                for index, (source, goal) in enumerate(zip(sources, target))
            ]
        )
    return waits


def rows_body(all_ref, gain1_ref, gain2_ref, *refs):
    parts1, parts2, refs = refs[:5], refs[5:10], refs[10:]
    result_ref, weight1_ref, weight2_ref, normed_ref, kv_ref, stream_ref, sems = refs[:7]
    mixing1, mixing2 = refs[7:12], refs[12:]
    chunks = all_ref.shape[0]
    inner = kv_ref.shape[1] // 2
    bands = lax.axis_size("band")
    band = lax.axis_index("band")
    core = lax.rem(lax.axis_index("batch"), 2)
    view = lax.axis_index("view")
    deep = lax.axis_size("view") // 2
    left = lax.rem(view, 2)
    own = jnp.where(view < deep, left, chunks - 1 - left)
    contract = (((1,), (1,)), ((), ()))
    waits1 = assembled(parts1, weight1_ref, sems.at[0], band, bands, core)
    waits2 = assembled(parts2, weight2_ref, sems.at[1], band, bands, core)
    project(all_ref, gain1_ref, waits1, weight1_ref, normed_ref, kv_ref)
    _, tokens, _ = all_ref.shape
    mixed(band >= 0, lambda: normed_ref[...], weight1_ref, kv_ref, *mixing1)
    waits1[3]()
    update = lax.dot_general(
        mixing1[-1][...], weight1_ref[:, 3 * inner :], contract, preferred_element_type=jnp.float32
    )
    for chunk in range(chunks):
        stream_ref[chunk] = (
            all_ref[chunk].astype(jnp.float32) + update[chunk * tokens : (chunk + 1) * tokens]
        ).astype(jnp.bfloat16)
    for part in range(4):
        waits2[part]()
    project(stream_ref, gain2_ref, None, weight2_ref, normed_ref, kv_ref)
    mixed(band >= 0, lambda: chunk_of(normed_ref, own, tokens), weight2_ref, kv_ref, *mixing2)
    update = lax.dot_general(
        mixing2[-1][...], weight2_ref[:, 3 * inner :], contract, preferred_element_type=jnp.float32
    )
    result_ref[...] = (stream_ref[own].astype(jnp.float32) + update).astype(jnp.bfloat16)


def rows_layer(everything, gain1, gain2, weights):
    chunks, tokens, width = everything.shape
    inner = weights[1].shape[1]
    count = chunks * tokens
    vmem = pl.BlockSpec(memory_space=pltpu.VMEM)
    hbm = pl.BlockSpec(memory_space=pltpu.HBM)
    return pl.pallas_call(
        rows_body,
        out_shape=jax.ShapeDtypeStruct((tokens, width), jnp.bfloat16),
        in_specs=[vmem] * 3 + [hbm] * 2 + [pl.BlockSpec(memory_space=pl.ANY)] * 3 + [hbm] * 5,
        out_specs=vmem,
        scratch_shapes=[
            pltpu.VMEM((width, 4 * inner), jnp.bfloat16),
            pltpu.VMEM((width, 4 * inner), jnp.bfloat16),
            pltpu.VMEM((count, width), jnp.bfloat16),
            pltpu.VMEM((count, 2 * inner), jnp.bfloat16),
            pltpu.VMEM((chunks, tokens, width), jnp.bfloat16),
            pltpu.SemaphoreType.DMA((2, 4, 4)),
        ]
        + mixing_scratch(count, count, inner)
        + mixing_scratch(tokens, count, inner),
        compiler_params=pltpu.CompilerParams(vmem_limit_bytes=32 << 20),
        cost_estimate=estimate(chunks, tokens, width, inner),
        name="rows",
    )(everything, gain1, gain2, *kept(*weights[:2]), *weights[2:5], *kept(*weights[5:]))


def exchanged(stream, rows, groups):
    tokens, width = stream.shape
    return lax.all_to_all(
        stream.reshape(rows, tokens // rows, width),
        "view",
        split_axis=0,
        concat_axis=0,
        tiled=True,
        axis_index_groups=groups,
    ).reshape(tokens, width)


def layers(
    images,
    frame_gain,
    frame_qkv,
    frame_out,
    row1_gain,
    row1_qkv,
    row1_out,
    row2_gain,
    row2_qkv,
    row2_out,
):
    _, row_count, col_count, width = images.shape
    tokens = row_count * col_count
    views = lax.axis_size("view")
    bands = lax.axis_size("band")
    batches = lax.axis_size("batch")
    share = views // row_count
    near = 2
    deep = views // near
    side = share // near
    spread = [
        [y * deep + h * side + l for h in range(row_count)] for y in range(near) for l in range(side)
    ]
    ring = [
        [h * side + l for l in range(side)] + [deep + h * side + l for l in reversed(range(side))]
        for h in range(row_count)
    ]
    siblings = [(i, i ^ 1) for i in range(batches)]
    turn = [
        (b * batches + c, ((b + 1 - 2 * (c % 2)) % bands) * batches + c)
        for b in range(bands)
        for c in range(batches)
    ]

    shards = (row1_qkv, row1_out.T, row2_qkv, row2_out.T)
    everything = lax.all_gather(images.reshape(tokens, width), "band", axis=0, tiled=False)
    everything, nears = lax.optimization_barrier((everything, pack_layer(shards)))

    both = ("band", "batch")
    nears = [lax.ppermute(near, both, turn) for near in nears]
    stream = frame_layer(everything, frame_gain, frame_qkv, frame_out)
    stream = exchanged(stream, row_count, spread)
    fars = [lax.ppermute(near, both, turn) for near in nears]
    others = [lax.ppermute(near, "batch", siblings) for near in nears]
    gain1 = row1_gain.reshape(1, width)
    gain2 = row2_gain.reshape(1, width)
    everything = lax.all_gather(stream, "view", axis=0, tiled=False, axis_index_groups=ring)
    stream = rows_layer(
        everything, gain1, gain2, (*shards[:2], nears[0], fars[0], others[0], *shards[2:], nears[1], fars[1], others[1])
    )
    stream = exchanged(stream, row_count, spread)
    return stream.reshape(images.shape)


def solution(mesh):
    in_specs = (
        P(("batch", "view"), "band", None, None),
        P(),
        P(),
        P(),
        P(),
        P("band", None),
        P(None, "band"),
        P(),
        P("band", None),
        P(None, "band"),
    )
    out_specs = P(("batch", "view"), "band", None, None)
    return jax.shard_map(layers, mesh=mesh, in_specs=in_specs, out_specs=out_specs, check_vma=False)
```

```python
import math

import jax
import jax.numpy as jnp
from jax import lax
from jax.experimental import pallas as pl
from jax.experimental.pallas import tpu as pltpu
from jax.sharding import PartitionSpec as P


HEAD_DIM = 64
EPSILON = 1e-06
PAIR = 2 * HEAD_DIM
SCALE = HEAD_DIM ** (-0.5) * math.log2(math.e)
NORM_ROWS = 32
PACK_PARTS = 4
SOFTMAX_ROWS = 32


def project(all_ref, gain_ref, waits, weight_ref, normed_ref, kv_ref):
    chunks, tokens, width = all_ref.shape
    inner = kv_ref.shape[1] // 2
    gain = gain_ref[...].reshape(1, width)
    for chunk in range(chunks):
        for start in range(0, tokens, NORM_ROWS):
            values = all_ref[chunk, start : start + NORM_ROWS].astype(jnp.float32)
            factor = lax.rsqrt(jnp.mean(values * values, axis=-1, keepdims=True) + EPSILON)
            at = chunk * tokens + start
            normed_ref[at : at + NORM_ROWS, :] = (values * factor * gain).astype(jnp.bfloat16)
    for part in range(2):
        if waits:
            waits[1 + part]()
        kv_ref[:, part * inner : (part + 1) * inner] = jnp.dot(
            normed_ref[...],
            weight_ref[:, (1 + part) * inner : (2 + part) * inner],
            preferred_element_type=jnp.float32,
        ).astype(jnp.bfloat16)
    if waits:
        waits[0]()


def mixed(fence, read_normed, weight_ref, kv_ref, query_ref, score_ref, rounded_ref, inverse_ref, attended_ref):
    count = attended_ref.shape[0]
    inner = kv_ref.shape[1] // 2
    pairs = inner // PAIR

    @pl.when(fence)
    def _():
        first = lax.broadcasted_iota(jnp.int32, (count, PAIR), 1) < HEAD_DIM
        zeros = jnp.zeros((count, PAIR), jnp.bfloat16)
        queries = (
            jnp.dot(read_normed(), weight_ref[:, :inner], preferred_element_type=jnp.float32) * SCALE
        ).astype(jnp.bfloat16)
        for pair in range(pairs):
            query = queries[:, pair * PAIR : (pair + 1) * PAIR]
            query_ref[pair, :count] = jnp.where(first, query, zeros)
            query_ref[pair, count:] = jnp.where(first, zeros, query)

    def score(pair):
        score_ref[pair % 2] = lax.dot_general(
            query_ref[pair],
            kv_ref[:, pair * PAIR : (pair + 1) * PAIR],
            (((1,), (1,)), ((), ())),
            preferred_element_type=jnp.float32,
        )

    def weigh(pair):
        slot = pair % 2
        for start in range(0, 2 * count, SOFTMAX_ROWS):
            rows = slice(start, start + SOFTMAX_ROWS)
            scores = score_ref[slot, rows]
            weights = jnp.exp2(scores - jnp.max(scores, axis=-1, keepdims=True))
            total = jnp.sum(weights, axis=-1, keepdims=True)
            rounded_ref[slot, rows] = weights.astype(jnp.bfloat16)
            inverse_ref[slot, rows] = jnp.broadcast_to(1.0 / total, (SOFTMAX_ROWS, PAIR))

    def mix(pair):
        slot = pair % 2
        first = lax.broadcasted_iota(jnp.int32, (count, PAIR), 1) < HEAD_DIM
        result = inverse_ref[slot] * jnp.dot(
            rounded_ref[slot],
            kv_ref[:, inner + pair * PAIR : inner + (pair + 1) * PAIR],
            preferred_element_type=jnp.float32,
        )
        attended_ref[:, pair * PAIR : (pair + 1) * PAIR] = jnp.where(
            first, result[:count], result[count:]
        ).astype(jnp.bfloat16)

    for stage in range(pairs + 2):

        @pl.when(fence)
        def _(stage=stage):
            if stage < pairs:
                score(stage)
            if 0 <= stage - 1 < pairs:
                weigh(stage - 1)
            if 0 <= stage - 2:
                mix(stage - 2)


def mixing_scratch(count, keys, inner):
    pairs = inner // PAIR
    return [
        pltpu.VMEM((pairs, 2 * count, PAIR), jnp.bfloat16),
        pltpu.VMEM((2, 2 * count, keys), jnp.float32),
        pltpu.VMEM((2, 2 * count, keys), jnp.bfloat16),
        pltpu.VMEM((2, 2 * count, PAIR), jnp.float32),
        pltpu.VMEM((count, inner), jnp.bfloat16),
    ]


def chunk_of(normed_ref, own, tokens):
    return normed_ref[pl.ds(pl.multiple_of(own * tokens, tokens), tokens), :]


def started(copies):
    for copy in copies:
        copy.start()

    def wait():
        for copy in copies:
            copy.wait()

    return wait


def pack_body(*refs):
    shards, nears, sems = refs[:4], refs[4:6], refs[6]
    columns = shards[0].shape[1]
    copies = []
    for layer in range(2):
        qkv, out = shards[2 * layer : 2 * layer + 2]
        rows = qkv.shape[0] // PACK_PARTS
        for part in range(PACK_PARTS):
            at = slice(part * rows, (part + 1) * rows)
            for index, (source, goal) in enumerate(
                ((qkv, nears[layer].at[at, :columns]), (out, nears[layer].at[at, columns:]))
            ):
                copies.append(
                    pltpu.make_async_copy(source.at[at, :], goal, sems.at[layer, part, index])
                )
    started(copies)()


def pack_layer(shards):
    qkv, out = shards[:2]
    return pl.pallas_call(
        pack_body,
        out_shape=(
            jax.ShapeDtypeStruct((qkv.shape[0], qkv.shape[1] + out.shape[1]), jnp.bfloat16),
        )
        * 2,
        in_specs=[pl.BlockSpec(memory_space=pltpu.HBM)] * 4,
        out_specs=(pl.BlockSpec(memory_space=pltpu.VMEM),) * 2,
        scratch_shapes=[pltpu.SemaphoreType.DMA((2, PACK_PARTS, 2))],
        compiler_params=pltpu.CompilerParams(vmem_limit_bytes=4 << 20),
        name="pack",
    )(*kept(*shards))


def frame_body(
    all_ref,
    gain_ref,
    weight_ref,
    out_ref,
    result_ref,
    mix_ref,
    normed_ref,
    kv_ref,
    sem,
    *mixing,
):
    band = lax.axis_index("band")
    mix = started([pltpu.make_async_copy(out_ref, mix_ref, sem)])
    project(all_ref, gain_ref, None, weight_ref, normed_ref, kv_ref)
    _, tokens, _ = all_ref.shape
    mixed(band >= 0, lambda: chunk_of(normed_ref, band, tokens), weight_ref, kv_ref, *mixing)
    mix()
    update = jnp.dot(mixing[-1][...], mix_ref[...], preferred_element_type=jnp.float32)
    result_ref[...] = (all_ref[band].astype(jnp.float32) + update).astype(jnp.bfloat16)


def kept(*arrays):
    return [pltpu.with_memory_space_constraint(array, pltpu.HBM) for array in arrays]


def frame_layer(everything, gain, qkv, out):
    chunks, tokens, width = everything.shape
    inner = out.shape[0]
    count = chunks * tokens
    vmem = pl.BlockSpec(memory_space=pltpu.VMEM)
    return pl.pallas_call(
        frame_body,
        out_shape=jax.ShapeDtypeStruct((tokens, width), jnp.bfloat16),
        in_specs=[vmem] * 3 + [pl.BlockSpec(memory_space=pltpu.HBM)],
        out_specs=vmem,
        scratch_shapes=[
            pltpu.VMEM((inner, width), jnp.bfloat16),
            pltpu.VMEM((count, width), jnp.bfloat16),
            pltpu.VMEM((count, 2 * inner), jnp.bfloat16),
            pltpu.SemaphoreType.DMA,
        ]
        + mixing_scratch(tokens, count, inner),
        compiler_params=pltpu.CompilerParams(vmem_limit_bytes=20 << 20),
        cost_estimate=estimate(chunks, tokens, width, inner),
        name="frame",
    )(everything, gain, qkv, *kept(out))


def estimate(chunks, tokens, width, inner):
    count = chunks * tokens
    return pl.CostEstimate(
        flops=4 * count * width * inner + 4 * tokens * width * inner + 4 * tokens * count * inner,
        bytes_accessed=2 * (count * width + 4 * width * inner),
        transcendentals=tokens * count * inner // HEAD_DIM,
    )


def assembled(parts, weight_ref, sems, band, bands, core):
    inner = parts[1].shape[1]
    rows = parts[1].shape[0]
    target = [
        pl.ds(pl.multiple_of(lax.rem(band + step, bands) * rows, rows), rows)
        for step in (0, bands - 1 + 2 * core, 2, 1 + 2 * core)
    ]
    waits = {}
    for order, part in enumerate((1, 2, 0, 3)):
        columns = slice(part * inner, (part + 1) * inner)
        sources = (parts[1] if part == 3 else parts[0].at[:, columns],)
        sources += tuple(ref.at[:, columns] for ref in parts[2:])
        waits[part] = started(
            [
                pltpu.make_async_copy(source, weight_ref.at[goal, columns], sems.at[order, index])
                for index, (source, goal) in enumerate(zip(sources, target))
            ]
        )
    return waits


def rows_body(all_ref, gain1_ref, gain2_ref, *refs):
    parts1, parts2, refs = refs[:5], refs[5:10], refs[10:]
    result_ref, weight1_ref, weight2_ref, normed_ref, kv_ref, stream_ref, sems = refs[:7]
    mixing1, mixing2 = refs[7:12], refs[12:]
    chunks = all_ref.shape[0]
    inner = kv_ref.shape[1] // 2
    bands = lax.axis_size("band")
    band = lax.axis_index("band")
    core = lax.rem(lax.axis_index("batch"), 2)
    view = lax.axis_index("view")
    deep = lax.axis_size("view") // 2
    left = lax.rem(view, 2)
    own = jnp.where(view < deep, left, chunks - 1 - left)
    contract = (((1,), (1,)), ((), ()))
    waits1 = assembled(parts1, weight1_ref, sems.at[0], band, bands, core)
    waits2 = assembled(parts2, weight2_ref, sems.at[1], band, bands, core)
    project(all_ref, gain1_ref, waits1, weight1_ref, normed_ref, kv_ref)
    _, tokens, _ = all_ref.shape
    mixed(band >= 0, lambda: normed_ref[...], weight1_ref, kv_ref, *mixing1)
    waits1[3]()
    update = lax.dot_general(
        mixing1[-1][...], weight1_ref[:, 3 * inner :], contract, preferred_element_type=jnp.float32
    )
    for chunk in range(chunks):
        stream_ref[chunk] = (
            all_ref[chunk].astype(jnp.float32) + update[chunk * tokens : (chunk + 1) * tokens]
        ).astype(jnp.bfloat16)
    for part in range(4):
        waits2[part]()
    project(stream_ref, gain2_ref, None, weight2_ref, normed_ref, kv_ref)
    mixed(band >= 0, lambda: chunk_of(normed_ref, own, tokens), weight2_ref, kv_ref, *mixing2)
    update = lax.dot_general(
        mixing2[-1][...], weight2_ref[:, 3 * inner :], contract, preferred_element_type=jnp.float32
    )
    result_ref[...] = (stream_ref[own].astype(jnp.float32) + update).astype(jnp.bfloat16)


def rows_layer(everything, gain1, gain2, weights):
    chunks, tokens, width = everything.shape
    inner = weights[1].shape[1]
    count = chunks * tokens
    vmem = pl.BlockSpec(memory_space=pltpu.VMEM)
    hbm = pl.BlockSpec(memory_space=pltpu.HBM)
    return pl.pallas_call(
        rows_body,
        out_shape=jax.ShapeDtypeStruct((tokens, width), jnp.bfloat16),
        in_specs=[vmem] * 3 + [hbm] * 2 + [pl.BlockSpec(memory_space=pl.ANY)] * 3 + [hbm] * 5,
        out_specs=vmem,
        scratch_shapes=[
            pltpu.VMEM((width, 4 * inner), jnp.bfloat16),
            pltpu.VMEM((width, 4 * inner), jnp.bfloat16),
            pltpu.VMEM((count, width), jnp.bfloat16),
            pltpu.VMEM((count, 2 * inner), jnp.bfloat16),
            pltpu.VMEM((chunks, tokens, width), jnp.bfloat16),
            pltpu.SemaphoreType.DMA((2, 4, 4)),
        ]
        + mixing_scratch(count, count, inner)
        + mixing_scratch(tokens, count, inner),
        compiler_params=pltpu.CompilerParams(vmem_limit_bytes=32 << 20),
        cost_estimate=estimate(chunks, tokens, width, inner),
        name="rows",
    )(everything, gain1, gain2, *kept(*weights[:2]), *weights[2:5], *kept(*weights[5:]))


def exchanged(stream, rows, groups):
    tokens, width = stream.shape
    return lax.all_to_all(
        stream.reshape(rows, tokens // rows, width),
        "view",
        split_axis=0,
        concat_axis=0,
        tiled=True,
        axis_index_groups=groups,
    ).reshape(tokens, width)


def layers(
    images,
    frame_gain,
    frame_qkv,
    frame_out,
    row1_gain,
    row1_qkv,
    row1_out,
    row2_gain,
    row2_qkv,
    row2_out,
):
    _, row_count, col_count, width = images.shape
    tokens = row_count * col_count
    views = lax.axis_size("view")
    bands = lax.axis_size("band")
    batches = lax.axis_size("batch")
    share = views // row_count
    near = 2
    deep = views // near
    side = share // near
    spread = [
        [y * deep + h * side + l for h in range(row_count)] for y in range(near) for l in range(side)
    ]
    ring = [
        [h * side + l for l in range(side)] + [deep + h * side + l for l in reversed(range(side))]
        for h in range(row_count)
    ]
    siblings = [(i, i ^ 1) for i in range(batches)]
    turn = [
        (b * batches + c, ((b + 1 - 2 * (c % 2)) % bands) * batches + c)
        for b in range(bands)
        for c in range(batches)
    ]

    shards = (row1_qkv, row1_out.T, row2_qkv, row2_out.T)
    everything = lax.all_gather(images.reshape(tokens, width), "band", axis=0, tiled=False)
    everything, nears = lax.optimization_barrier((everything, pack_layer(shards)))

    both = ("band", "batch")
    nears = [lax.ppermute(near, both, turn) for near in nears]
    stream = frame_layer(everything, frame_gain, frame_qkv, frame_out)
    stream = exchanged(stream, row_count, spread)
    fars = [lax.ppermute(near, both, turn) for near in nears]
    others = [lax.ppermute(near, "batch", siblings) for near in nears]
    gain1 = row1_gain.reshape(1, width)
    gain2 = row2_gain.reshape(1, width)
    everything = lax.all_gather(stream, "view", axis=0, tiled=False, axis_index_groups=ring)
    stream = rows_layer(
        everything, gain1, gain2, (*shards[:2], nears[0], fars[0], others[0], *shards[2:], nears[1], fars[1], others[1])
    )
    stream = exchanged(stream, row_count, spread)
    return stream.reshape(images.shape)


def solution(mesh):
    in_specs = (
        P(("batch", "view"), "band", None, None),
        P(),
        P(),
        P(),
        P(),
        P("band", None),
        P(None, "band"),
        P(),
        P("band", None),
        P(None, "band"),
    )
    out_specs = P(("batch", "view"), "band", None, None)
    return jax.shard_map(layers, mesh=mesh, in_specs=in_specs, out_specs=out_specs, check_vma=False)
```
